256 devices in a mesh: space: 64 (over z, y, core), tm: 4 (over x).
Axes of the slice: x: 4, y: 4, z: 8, core: 2. Of those that a mesh axis runs over, the one named last changes fastest.
Arguments:
- snapshots: bfloat16 [256, 524288], P('tm', 'space'), may hold values from -75 to 75
- prior_basis: bfloat16 [256, 524288], P('tm', 'space'), may hold values from -75 to 75
- mass_factor: bfloat16 [7, 64, 524288], P(None, None, 'space'), may hold values from -1 to 3.2, as said below
- neighbours: int32 [8192, 7], P('space'), may hold values from 0 to 8191, as said below
Outputs:
- merged_basis: bfloat16 [64, 524288], P(None, ('space', 'tm'))
- merged_weighted: bfloat16 [64, 524288], P(None, ('space', 'tm'))
The draws below stay inside these ranges and needn't reach their ends.
Inputs may be any that keep to these rules, and one draw needn't show every extreme that they name: `mass_factor`: factor entries; the diagonal of each block's own coupling lies in 1.5 to 3. neighbours[i, 0] = i; every entry lies within 8 blocks of i; in every draw some entries lie exactly 8 blocks below and above their block.
All inputs are finite; a program needn't handle non-finite values.
Results may differ from the reference program's by a relative error of at most 0.018.
Values may be sent and summed in bfloat16 or wider, within the bound.
A program may use at most 128 MiB of HBM per device.

```python
import math
import jax
import jax.numpy as jnp
from jax import lax

BLOCK_DOFS = 64
RANK = 64
SNAPSHOTS = 64
NEIGHBOURS = 7
REACH = 8
SUBSPACE_STEPS = 3
LOCAL_BLOCKS = 128
BLOCKS = 8192
DOFS = 524288
TIME_SNAPSHOTS = 256
TIME_RANKS = 256
N_SPACE = 64
N_TM = 4


def scaled_rows(key, count, low, high):
    key_column, key_rough, key_entries = jax.random.split(key, 3)
    column_scale = jnp.exp(jax.random.uniform(key_column, (count, 1), jnp.float32, math.log(low), math.log(high)))
    position = jnp.arange(DOFS, dtype=jnp.float32) / DOFS
    roughness = jnp.exp(jax.random.uniform(key_rough, (1, DOFS), jnp.float32, math.log(0.5), math.log(2.0)))
    row_scale = jnp.power(3.0, position)[None, :] * roughness
    entries = jnp.clip(jax.random.normal(key_entries, (count, DOFS), jnp.float32), -4.0, 4.0)
    return entries * column_scale * row_scale


def draw_snapshots(key, part):
    return scaled_rows(jax.random.fold_in(key, 11), TIME_SNAPSHOTS, 0.3, 3.0).astype(jnp.bfloat16)


def draw_prior_basis(key, part):
    return scaled_rows(jax.random.fold_in(key, 23), TIME_RANKS, 0.3, 3.0).astype(jnp.bfloat16)


def draw_mass_factor(key, part):
    key_couple, key_diagonal = jax.random.split(jax.random.fold_in(key, 37), 2)
    spread = 1.0 / math.sqrt(BLOCK_DOFS * NEIGHBOURS)
    couples = jnp.clip(jax.random.normal(key_couple, (NEIGHBOURS, BLOCK_DOFS, DOFS), jnp.float32), -4.0, 4.0) * spread
    diagonal_values = jnp.exp(jax.random.uniform(key_diagonal, (DOFS,), jnp.float32, math.log(1.5), math.log(3.0)))
    row_place = jnp.arange(DOFS) % BLOCK_DOFS
    column_place = jnp.arange(BLOCK_DOFS)
    slot_index = jnp.arange(NEIGHBOURS)
    on_diagonal = (slot_index[:, None, None] == 0) & (column_place[None, :, None] == row_place[None, None, :])
    return jnp.where(on_diagonal, diagonal_values[None, None, :], couples).astype(jnp.bfloat16)


def draw_neighbours(key, part):
    offsets = jax.random.randint(jax.random.fold_in(key, 41), (BLOCKS, NEIGHBOURS), -REACH, REACH + 1)
    block_index = jnp.arange(BLOCKS, dtype=jnp.int32)[:, None]
    slot_index = jnp.arange(NEIGHBOURS, dtype=jnp.int32)[None, :]
    offsets = jnp.where(slot_index == 0, 0, offsets)
    position = block_index % LOCAL_BLOCKS
    offsets = jnp.where((slot_index == 1) & (position == 0), -REACH, offsets)
    offsets = jnp.where((slot_index == 1) & (position == LOCAL_BLOCKS - 1), REACH, offsets)
    return jnp.clip(block_index + offsets, 0, BLOCKS - 1).astype(jnp.int32)


def setup_inputs(seed: int = 0) -> dict:
    streams_of = jax.random.split(jax.random.key(seed), 5)
    snapshots = draw_snapshots(jax.random.fold_in(streams_of[4], 71), 0)
    prior_basis = draw_prior_basis(jax.random.fold_in(streams_of[4], 71), 0)
    mass_factor = draw_mass_factor(jax.random.fold_in(streams_of[4], 71), 0)
    neighbours = draw_neighbours(jax.random.fold_in(streams_of[4], 71), 0)
    return {"snapshots": snapshots, "prior_basis": prior_basis, "mass_factor": mass_factor, "neighbours": neighbours}


def weigh_rows(stacked, mass_factor, neighbours):
    columns = stacked.shape[0]
    blocks = stacked.reshape(columns, BLOCKS, BLOCK_DOFS)

    def one_slab(slab_index):
        first_row = slab_index * LOCAL_BLOCKS
        slab_rows = lax.dynamic_slice_in_dim(neighbours, first_row, LOCAL_BLOCKS, 0)
        picked = jnp.take(blocks, slab_rows, axis=1).astype(jnp.float32)
        factor = lax.dynamic_slice_in_dim(mass_factor, first_row * BLOCK_DOFS, LOCAL_BLOCKS * BLOCK_DOFS, 2)
        factor = factor.reshape(NEIGHBOURS, BLOCK_DOFS, LOCAL_BLOCKS, BLOCK_DOFS).astype(jnp.float32)
        return jnp.einsum('cbkq,kqbr->cbr', picked, factor).astype(jnp.bfloat16)
    slabs = lax.map(one_slab, jnp.arange(N_SPACE, dtype=jnp.int32))
    return jnp.transpose(slabs, (1, 0, 2, 3)).reshape(columns, DOFS)

def compress(gram_total):
    highest = lax.Precision.HIGHEST
    order_size = gram_total.shape[0]
    weights = jnp.eye(order_size, RANK, dtype=jnp.float32)
    for repeat in range(SUBSPACE_STEPS):
        product = jnp.dot(gram_total, weights, precision=highest)
        inner_gram = jnp.dot(product.T, jnp.dot(gram_total, product, precision=highest), precision=highest)
        scales = jnp.sqrt(jnp.diagonal(inner_gram))
        factor_lower = jnp.linalg.cholesky(inner_gram / (scales[:, None] * scales[None, :]))
        normed = product / scales[None, :]
        weights = lax.linalg.triangular_solve(factor_lower, normed, left_side=False, lower=True, transpose_a=True)
    product = jnp.dot(gram_total, weights, precision=highest)
    lengths = jnp.sqrt(lax.optimization_barrier(jnp.sum(product * product, axis=0)) + 1e-06)
    return (weights * lengths[None, :]).astype(jnp.bfloat16)

def reduce_pair(stacked, weighted):
    gram_total = jnp.dot(weighted.astype(jnp.float32), weighted.T.astype(jnp.float32), preferred_element_type=jnp.float32)
    coefficients = compress(gram_total)
    basis = jnp.dot(coefficients.T.astype(jnp.float32), stacked.astype(jnp.float32), preferred_element_type=jnp.float32).astype(jnp.bfloat16)
    weighted_basis = jnp.dot(coefficients.T.astype(jnp.float32), weighted.astype(jnp.float32), preferred_element_type=jnp.float32).astype(jnp.bfloat16)
    return (basis, weighted_basis)

def reference(snapshots, prior_basis, mass_factor, neighbours):
    groups = []
    for member in range(N_TM):
        stacked = jnp.concatenate([prior_basis[member * RANK:(member + 1) * RANK], snapshots[member * SNAPSHOTS:(member + 1) * SNAPSHOTS]], axis=0)
        groups.append(reduce_pair(stacked, weigh_rows(stacked, mass_factor, neighbours)))
    stride = 1
    while stride < N_TM:
        merged = list(groups)
        for member in range(N_TM):
            if member % (2 * stride) < stride:
                lower_pair = groups[member]
                upper_pair = groups[member + stride]
                stacked = jnp.concatenate([lower_pair[0], upper_pair[0]], axis=0)
                weighted = jnp.concatenate([lower_pair[1], upper_pair[1]], axis=0)
                result = reduce_pair(stacked, weighted)
                merged[member] = result
                merged[member + stride] = result
        groups = merged
        stride = stride * 2
    return (groups[0][0], groups[0][1])
```

```python
import functools

import jax
import jax.numpy as jnp
from jax import lax
from jax.experimental import pallas as pl
from jax.experimental.pallas import tpu as pltpu
from jax.sharding import PartitionSpec as P

BLOCK = 64
RANK = 64
NEIGHBOURS = 7
REACH = 8
STEPS = 3
LOCAL_BLOCKS = 128
N_SPACE = 64
N_TM = 4
ROWS = 128
SLAB = LOCAL_BLOCKS * BLOCK
SHARE = SLAB // N_TM
HALO = REACH * BLOCK
WINDOW = SHARE + 2 * HALO
SHARE_BLOCKS = SHARE // BLOCK
TILES = WINDOW // 128
MESH = pl.DeviceIdType.MESH
HIGHEST = lax.Precision.HIGHEST
F32 = jnp.float32
BF16 = jnp.bfloat16


def dot_nn(a, b):
    return lax.dot_general(
        a, b, (((1,), (0,)), ((), ())), precision=HIGHEST, preferred_element_type=F32
    )


def dot_nt(a, b):
    return lax.dot_general(
        a, b, (((1,), (1,)), ((), ())), precision=HIGHEST, preferred_element_type=F32
    )


def span(target):
    low = max(0, SHARE * target - HALO)
    high = min(SLAB, SHARE * (target + 1) + HALO)
    return low, high - low, low - (SHARE * target - HALO)


def exchange_kernel(prior, snaps, out, bounce, send_sem, recv_sem, halo_send, halo_recv, local_sem):
    s = lax.axis_index("space")
    t = lax.axis_index("tm")
    up = lax.rem(s + 1, N_SPACE)
    down = lax.rem(s + N_SPACE - 1, N_SPACE)
    barrier = pltpu.get_barrier_semaphore()
    for g in range(N_TM):

        @pl.when(t != g)
        def _():
            pl.semaphore_signal(barrier, inc=1, device_id=(s, g), device_id_type=MESH)

        @pl.when(t == 0)
        def _():
            pl.semaphore_signal(barrier, inc=1, device_id=(down, g), device_id_type=MESH)

        @pl.when(t == N_TM - 1)
        def _():
            pl.semaphore_signal(barrier, inc=1, device_id=(up, g), device_id_type=MESH)

    pl.semaphore_wait(barrier, N_TM + 1)
    sources = (prior, snaps)

    def rows_of(group, part):
        return pl.ds(pl.multiple_of(group * ROWS + part * 64, 64), 64)

    def halo(part, side):
        low = SLAB - HALO if side == 0 else 0
        at = 0 if side == 0 else WINDOW - HALO
        return pltpu.make_async_remote_copy(
            src_ref=sources[part].at[:, pl.ds(low, HALO)],
            dst_ref=out.at[rows_of(t, part), pl.ds(at, HALO)],
            send_sem=halo_send.at[side, part],
            recv_sem=halo_recv.at[t, part],
            device_id=(up, 0) if side == 0 else (down, N_TM - 1),
            device_id_type=MESH,
        )

    def share(part, target):
        low, width, at = span(target)
        return pltpu.make_async_remote_copy(
            src_ref=sources[part].at[:, pl.ds(low, width)],
            dst_ref=out.at[rows_of(t, part), pl.ds(at, width)],
            send_sem=send_sem.at[target, part],
            recv_sem=recv_sem.at[t, part],
            device_id=(s, target),
            device_id_type=MESH,
        )

    def load(part, target):
        low, width, at = span(target)
        return pltpu.make_async_copy(
            sources[part].at[:, pl.ds(low, width)],
            bounce.at[pl.ds(part * 64, 64), pl.ds(at, width)],
            local_sem.at[part],
        )

    def store(part, target):
        low, width, at = span(target)
        return pltpu.make_async_copy(
            bounce.at[pl.ds(part * 64, 64), pl.ds(at, width)],
            out.at[pl.ds(target * ROWS + part * 64, 64), pl.ds(at, width)],
            local_sem.at[2 + part],
        )

    for own in range(N_TM):

        @pl.when(t == own)
        def _():
            for hop in (2, 1, 3):
                for part in range(2):
                    share(part, (own + hop) % N_TM).start()

    for part in range(2):
        for side in range(2):
            halo(part, side).start()
    for own in range(N_TM):

        @pl.when(t == own)
        def _():
            for part in range(2):
                load(part, own).start()
            for part in range(2):
                load(part, own).wait()
                store(part, own).start()
            for part in range(2):
                store(part, own).wait()
            low, width, at = span(own)
            for part in range(2):
                for hop in (1, 3, 2):
                    g = (own + hop) % N_TM
                    pltpu.make_async_remote_copy(
                        src_ref=sources[part].at[:, pl.ds(low, width)],
                        dst_ref=out.at[pl.ds(g * ROWS + part * 64, 64), pl.ds(at, width)],
                        send_sem=send_sem.at[own, part],
                        recv_sem=recv_sem.at[g, part],
                        device_id=(s, own),
                        device_id_type=MESH,
                    ).wait_recv()
                    share(part, g).wait_send()
            if own in (0, N_TM - 1):
                at = 0 if own == 0 else WINDOW - HALO
                for part in range(2):
                    for g in range(N_TM):
                        pltpu.make_async_remote_copy(
                            src_ref=sources[part].at[:, pl.ds(0, HALO)],
                            dst_ref=out.at[pl.ds(g * ROWS + part * 64, 64), pl.ds(at, HALO)],
                            send_sem=halo_send.at[0, part],
                            recv_sem=halo_recv.at[g, part],
                            device_id=(s, own),
                            device_id_type=MESH,
                        ).wait_recv()

    for part in range(2):
        for side in range(2):
            halo(part, side).wait_send()


def exchange(prior, snaps):
    return pl.pallas_call(
        exchange_kernel,
        out_shape=jax.ShapeDtypeStruct((N_TM * ROWS, WINDOW), BF16),
        in_specs=[pl.BlockSpec(memory_space=pl.ANY)] * 2,
        out_specs=pl.BlockSpec(memory_space=pl.ANY),
        scratch_shapes=[
            pltpu.VMEM((ROWS, WINDOW), BF16),
            pltpu.SemaphoreType.DMA((N_TM, 2)),
            pltpu.SemaphoreType.DMA((N_TM, 2)),
            pltpu.SemaphoreType.DMA((2, 2)),
            pltpu.SemaphoreType.DMA((N_TM, 2)),
            pltpu.SemaphoreType.DMA((4,)),
        ],
        compiler_params=pltpu.CompilerParams(collective_id=0, has_side_effects=True),
        name="exchange",
    )(prior, snaps)


def weigh_kernel(place, nb, x, mass, w, gram, shifted, factor, picked, sem):
    s, t = place[0], place[1]
    fetch = pltpu.make_async_copy(
        mass.at[:, :, pl.ds(pl.multiple_of(t * SHARE, 128), SHARE)], factor, sem
    )
    fetch.start()
    first = s * LOCAL_BLOCKS + t * SHARE_BLOCKS - REACH
    lane = lax.broadcasted_iota(jnp.int32, (1, 128), 1)
    in_low = lane < BLOCK
    for m in range(TILES + 1):
        before = x[:, pl.ds(128 * max(m - 1, 0), 128)]
        after = x[:, pl.ds(128 * min(m, TILES - 1), 128)]
        shifted[:, pl.ds(128 * m, 128)] = jnp.concatenate(
            [before[:, BLOCK:], after[:, :BLOCK]], axis=1
        )
    fetch.wait()

    def one_tile(j, carry):
        zero = jnp.zeros((BLOCK, 128), BF16)
        pieces = []
        for k in range(NEIGHBOURS):
            n_low = nb[(2 * j) * NEIGHBOURS + k] - first
            n_high = nb[(2 * j + 1) * NEIGHBOURS + k] - first
            odd_low = lax.rem(n_low, 2)
            odd_high = lax.rem(n_high, 2)
            low_at = pl.multiple_of(((n_low + 1) // 2) * 128, 128)
            high_at = pl.multiple_of((n_high // 2) * 128, 128)

            @pl.when(odd_low == 0)
            def _():
                picked[:, pl.ds(128 * k, 128)] = x[:, pl.ds(low_at, 128)]

            @pl.when(odd_low == 1)
            def _():
                picked[:, pl.ds(128 * k, 128)] = shifted[:, pl.ds(low_at, 128)]

            @pl.when(odd_high == 1)
            def _():
                picked[:, pl.ds(128 * k, 128)] = jnp.where(
                    in_low, picked[:, pl.ds(128 * k, 128)], x[:, pl.ds(high_at, 128)]
                )

            @pl.when(odd_high == 0)
            def _():
                picked[:, pl.ds(128 * k, 128)] = jnp.where(
                    in_low, picked[:, pl.ds(128 * k, 128)], shifted[:, pl.ds(high_at, 128)]
                )

            block = factor[k, :, pl.ds(pl.multiple_of(j * 128, 128), 128)]
            pieces.append(jnp.where(in_low, block, zero))
            pieces.append(jnp.where(in_low, zero, block))
        result = jnp.dot(
            picked[...], jnp.concatenate(pieces, axis=0), preferred_element_type=F32
        )
        w[:, pl.ds(pl.multiple_of(j * 128, 128), 128)] = result.astype(BF16)
        return carry

    lax.fori_loop(0, SHARE_BLOCKS // 2, one_tile, 0)
    at = 0
    for a in range(N_TM):
        for b in range(a, N_TM):
            gram[at] = lax.dot_general(
                w[pl.ds(a * ROWS, ROWS), :],
                w[pl.ds(b * ROWS, ROWS), :],
                (((1,), (1,)), ((), ())),
                preferred_element_type=F32,
            )
            at += 1


def weigh(place, nb, x, mass):
    rows = N_TM * ROWS
    return pl.pallas_call(
        weigh_kernel,
        out_shape=(
            jax.ShapeDtypeStruct((rows, SHARE), BF16),
            jax.ShapeDtypeStruct((10, ROWS, ROWS), F32),
        ),
        in_specs=[
            pl.BlockSpec(memory_space=pltpu.SMEM),
            pl.BlockSpec(memory_space=pltpu.SMEM),
            pl.BlockSpec(memory_space=pltpu.VMEM),
            pl.BlockSpec(memory_space=pl.ANY),
        ],
        out_specs=(
            pl.BlockSpec(memory_space=pltpu.VMEM),
            pl.BlockSpec(memory_space=pltpu.VMEM),
        ),
        scratch_shapes=[
            pltpu.VMEM((rows, (TILES + 1) * 128), BF16),
            pltpu.VMEM((NEIGHBOURS, BLOCK, SHARE), BF16),
            pltpu.VMEM((rows, NEIGHBOURS * 128), BF16),
            pltpu.SemaphoreType.DMA,
        ],
        name="weigh",
    )(place, nb, x, mass)


PIECE = 40


def reduce_kernel(inp, out, half, r_core, s_x, r_x, s_y, r_y, r_z, send_sem, recv_sem):
    s = lax.axis_index("space")
    x = lax.axis_index("tm")
    c = lax.rem(s, 2)
    y = lax.rem(s // 2, 4)
    z = s // 8

    def space_of(zz, yy, cc):
        return zz * 8 + yy * 2 + cc

    core_peer = (space_of(z, y, 1 - c), x)
    x_peers = [(s, lax.rem(x + d, 4)) for d in (1, 2, 3)]
    y_peers = [(space_of(z, lax.rem(y + d, 4), c), x) for d in (1, 2, 3)]
    z_peers = [(space_of(lax.rem(z + d, 8), y, c), x) for d in range(1, 8)]
    barrier = pltpu.get_barrier_semaphore()
    for peer in [core_peer] + x_peers + y_peers + z_peers:
        pl.semaphore_signal(barrier, inc=1, device_id=peer, device_id_type=MESH)
    pl.semaphore_wait(barrier, 14)

    def copy(src, dst, slot, peer):
        return pltpu.make_async_remote_copy(
            src_ref=src,
            dst_ref=dst,
            send_sem=send_sem.at[slot],
            recv_sem=recv_sem.at[slot],
            device_id=peer,
            device_id_type=MESH,
        )

    def run(copies):
        for one in copies:
            one.start()
        for one in copies:
            one.wait()

    run([copy(inp.at[1 - c], r_core, 0, core_peer)])
    half[...] = inp[c] + r_core[...]
    run(
        [
            copy(half.at[lax.rem(x + d, 4)], r_x.at[d - 1], d, x_peers[d - 1])
            for d in (2, 1, 3)
        ]
    )
    s_x[...] = half[x] + r_x[0] + r_x[1] + r_x[2]
    run(
        [
            copy(s_x.at[lax.rem(y + d, 4)], r_y.at[d - 1], 3 + d, y_peers[d - 1])
            for d in (2, 1, 3)
        ]
    )
    r_z[z] = s_x[y] + r_y[0] + r_y[1] + r_y[2]
    run([copy(r_z.at[z], r_z.at[z], 6 + d, z_peers[d - 1]) for d in (4, 3, 5, 2, 6, 1, 7)])
    total = r_z[0]
    for i in range(1, 8):
        total = total + r_z[i]
    out[c, x, y] = total
    run([copy(out.at[c, x, y], out.at[c, x, y], 13 + d, y_peers[d - 1]) for d in (2, 1, 3)])
    run([copy(out.at[c, x], out.at[c, x], 16 + d, x_peers[d - 1]) for d in (2, 1, 3)])
    run([copy(out.at[c], out.at[c], 20, core_peer)])


def all_reduce(gram):
    shape = (2, 4, 4, PIECE, 128)
    return pl.pallas_call(
        reduce_kernel,
        out_shape=jax.ShapeDtypeStruct(shape, F32),
        in_specs=[pl.BlockSpec(memory_space=pltpu.VMEM)],
        out_specs=pl.BlockSpec(memory_space=pltpu.VMEM),
        scratch_shapes=[
            pltpu.VMEM(shape[1:], F32),
            pltpu.VMEM(shape[1:], F32),
            pltpu.VMEM(shape[2:], F32),
            pltpu.VMEM((3,) + shape[2:], F32),
            pltpu.VMEM((1, PIECE, 128), F32),
            pltpu.VMEM((3, PIECE, 128), F32),
            pltpu.VMEM((8, PIECE, 128), F32),
            pltpu.SemaphoreType.DMA((21,)),
            pltpu.SemaphoreType.DMA((21,)),
        ],
        compiler_params=pltpu.CompilerParams(collective_id=1, has_side_effects=True),
        name="all_reduce",
    )(gram.reshape(shape)).reshape(10, ROWS, ROWS)


def eliminate(inners):
    sub = lax.broadcasted_iota(jnp.int32, (8, 128), 0)
    lane = lax.broadcasted_iota(jnp.int32, (8, 128), 1)
    grids = []
    for inner in inners:
        tiles = []
        for i in range(8):
            unit = jnp.where(lane == 8 * i + sub + BLOCK, 1.0, 0.0).astype(F32)
            left = jnp.concatenate([inner[8 * i : 8 * i + 8, :], jnp.zeros((8, BLOCK), F32)], axis=1)
            tiles.append(left + unit)
        grids.append(tiles)
    roots = [[] for _ in inners]
    for j in range(BLOCK):
        here, inside = divmod(j, 8)
        for tiles, root in zip(grids, roots):
            cols = [
                jnp.broadcast_to(tiles[i][:, j : j + 1], (8, 128)) for i in range(here, 8)
            ]
            pivot = jnp.broadcast_to(cols[0][inside : inside + 1, :], (8, 128))
            row = jnp.broadcast_to(tiles[here][inside : inside + 1, :], (8, 128)) * (1.0 / pivot)
            if inside == 0:
                root.append(pivot)
            else:
                root[here] = jnp.where(sub == inside, pivot, root[here])
            for i in range(here, 8):
                change = cols[i - here] * row
                if i == here:
                    change = jnp.where(sub > inside, change, 0.0)
                tiles[i] = tiles[i] - change
    return [
        jnp.concatenate([tile * lax.rsqrt(d) for tile, d in zip(tiles, root)], axis=0)
        for tiles, root in zip(grids, roots)
    ]


def compress(grams):
    rows = [gram[:RANK, :] for gram in grams]
    products = rows
    zeros = jnp.zeros((BLOCK, ROWS), F32)

    def step(products):
        seconds = [dot_nn(p, g) for p, g in zip(products, grams)]
        inners = [dot_nt(p, q) for p, q in zip(products, seconds)]
        inverses = eliminate(inners)
        nexts = [
            dot_nn(inv, jnp.concatenate([zeros, q], axis=0)) for inv, q in zip(inverses, seconds)
        ]
        return inverses, nexts

    for _ in range(STEPS - 1):
        _, products = step(products)
    inverses, nexts = step(products)
    result = []
    for inv, p, q in zip(inverses, products, nexts):
        weights = dot_nn(inv, jnp.concatenate([zeros, p], axis=0))
        lengths = jnp.sqrt(jnp.sum(q * q, axis=1, keepdims=True) + 1e-06)
        result.append((weights * lengths).astype(BF16).astype(F32))
    return result


def merge_kernel(gram, out, full, below, middle, above):
    index = {}
    for a in range(N_TM):
        for b in range(a, N_TM):
            index[a, b] = len(index)
    for (a, b), at in index.items():
        block = gram[at]
        full[pl.ds(a * ROWS, ROWS), pl.ds(b * ROWS, ROWS)] = block
        if a != b:
            full[pl.ds(b * ROWS, ROWS), pl.ds(a * ROWS, ROWS)] = block.T
    below[...] = jnp.zeros_like(below)
    above[...] = jnp.zeros_like(above)
    lowest = compress([gram[index[g, g]] for g in range(N_TM)])
    for g in range(N_TM):
        below[pl.ds(g * RANK, RANK), pl.ds(g * ROWS, ROWS)] = lowest[g]
    for p in range(2):
        half = [
            dot_nn(lowest[g], full[pl.ds(g * ROWS, ROWS), pl.ds(2 * p * ROWS, 2 * ROWS)])
            for g in range(N_TM)
        ]
        middle[:, pl.ds(p * ROWS, ROWS)] = dot_nt(
            jnp.concatenate(half, axis=0),
            below[pl.ds(2 * p * RANK, 2 * RANK), pl.ds(2 * p * ROWS, 2 * ROWS)],
        )
    second = compress([middle[pl.ds(p * ROWS, ROWS), pl.ds(p * ROWS, ROWS)] for p in range(2)])
    for p in range(2):
        above[pl.ds(p * RANK, RANK), pl.ds(p * ROWS, ROWS)] = second[p]
    half = [dot_nn(second[p], middle[pl.ds(p * ROWS, ROWS), :]) for p in range(2)]
    last = compress([dot_nt(jnp.concatenate(half, axis=0), above[...])])[0]
    out[...] = dot_nn(dot_nn(last, above[...]), below[...]).astype(BF16)


def merge(gram):
    return pl.pallas_call(
        merge_kernel,
        out_shape=jax.ShapeDtypeStruct((RANK, N_TM * ROWS), BF16),
        in_specs=[pl.BlockSpec(memory_space=pltpu.VMEM)],
        out_specs=pl.BlockSpec(memory_space=pltpu.VMEM),
        scratch_shapes=[
            pltpu.VMEM((N_TM * ROWS, N_TM * ROWS), F32),
            pltpu.VMEM((N_TM * RANK, N_TM * ROWS), F32),
            pltpu.VMEM((N_TM * RANK, N_TM * RANK), F32),
            pltpu.VMEM((2 * RANK, 2 * ROWS), F32),
        ],
        name="merge",
    )(gram)


def shards(snapshots, prior_basis, mass_factor, neighbours):
    s = lax.axis_index("space")
    t = lax.axis_index("tm")
    place = jnp.stack([s, t]).astype(jnp.int32)
    nb = lax.dynamic_slice_in_dim(neighbours, t * SHARE_BLOCKS, SHARE_BLOCKS, 0).reshape(-1)
    x = exchange(prior_basis, snapshots)
    w, gram = weigh(place, nb, x, mass_factor)
    coefficients = merge(all_reduce(gram))
    own = lax.slice_in_dim(x, HALO, HALO + SHARE, axis=1)
    basis = jnp.dot(coefficients, own, preferred_element_type=F32).astype(BF16)
    weighted = jnp.dot(coefficients, w, preferred_element_type=F32).astype(BF16)
    return basis, weighted


def solution(mesh):
    return jax.shard_map(
        shards,
        mesh=mesh,
        in_specs=(P("tm", "space"), P("tm", "space"), P(None, None, "space"), P("space", None)),
        out_specs=(P(None, ("space", "tm")), P(None, ("space", "tm"))),
        check_vma=False,
    )
```

```python
import functools

import jax
import jax.numpy as jnp
from jax import lax
from jax.experimental import pallas as pl
from jax.experimental.pallas import tpu as pltpu
from jax.sharding import PartitionSpec as P

BLOCK = 64
RANK = 64
NEIGHBOURS = 7
REACH = 8
STEPS = 3
LOCAL_BLOCKS = 128
N_SPACE = 64
N_TM = 4
ROWS = 128
SLAB = LOCAL_BLOCKS * BLOCK
SHARE = SLAB // N_TM
HALO = REACH * BLOCK
WINDOW = SHARE + 2 * HALO
SHARE_BLOCKS = SHARE // BLOCK
TILES = WINDOW // 128
MESH = pl.DeviceIdType.MESH
HIGHEST = lax.Precision.HIGHEST
F32 = jnp.float32
BF16 = jnp.bfloat16


def dot_nn(a, b):
    return lax.dot_general(
        a, b, (((1,), (0,)), ((), ())), precision=HIGHEST, preferred_element_type=F32
    )


def dot_nt(a, b):
    return lax.dot_general(
        a, b, (((1,), (1,)), ((), ())), precision=HIGHEST, preferred_element_type=F32
    )


def span(target):
    low = max(0, SHARE * target - HALO)
    high = min(SLAB, SHARE * (target + 1) + HALO)
    return low, high - low, low - (SHARE * target - HALO)


def exchange_kernel(prior, snaps, out, bounce, send_sem, recv_sem, halo_send, halo_recv, local_sem):
    s = lax.axis_index("space")
    t = lax.axis_index("tm")
    up = lax.rem(s + 1, N_SPACE)
    down = lax.rem(s + N_SPACE - 1, N_SPACE)
    barrier = pltpu.get_barrier_semaphore()
    for g in range(N_TM):

        @pl.when(t != g)
        def _():
            pl.semaphore_signal(barrier, inc=1, device_id=(s, g), device_id_type=MESH)

        @pl.when(t == 0)
        def _():
            pl.semaphore_signal(barrier, inc=1, device_id=(down, g), device_id_type=MESH)

        @pl.when(t == N_TM - 1)
        def _():
            pl.semaphore_signal(barrier, inc=1, device_id=(up, g), device_id_type=MESH)

    pl.semaphore_wait(barrier, N_TM + 1)
    sources = (prior, snaps)

    def rows_of(group, part):
        return pl.ds(pl.multiple_of(group * ROWS + part * 64, 64), 64)

    def halo(part, side):
        low = SLAB - HALO if side == 0 else 0
        at = 0 if side == 0 else WINDOW - HALO
        return pltpu.make_async_remote_copy(
            src_ref=sources[part].at[:, pl.ds(low, HALO)],
            dst_ref=out.at[rows_of(t, part), pl.ds(at, HALO)],
            send_sem=halo_send.at[side, part],
            recv_sem=halo_recv.at[t, part],
            device_id=(up, 0) if side == 0 else (down, N_TM - 1),
            device_id_type=MESH,
        )

    def share(part, target):
        low, width, at = span(target)
        return pltpu.make_async_remote_copy(
            src_ref=sources[part].at[:, pl.ds(low, width)],
            dst_ref=out.at[rows_of(t, part), pl.ds(at, width)],
            send_sem=send_sem.at[target, part],
            recv_sem=recv_sem.at[t, part],
            device_id=(s, target),
            device_id_type=MESH,
        )

    def load(part, target):
        low, width, at = span(target)
        return pltpu.make_async_copy(
            sources[part].at[:, pl.ds(low, width)],
            bounce.at[pl.ds(part * 64, 64), pl.ds(at, width)],
            local_sem.at[part],
        )

    def store(part, target):
        low, width, at = span(target)
        return pltpu.make_async_copy(
            bounce.at[pl.ds(part * 64, 64), pl.ds(at, width)],
            out.at[pl.ds(target * ROWS + part * 64, 64), pl.ds(at, width)],
            local_sem.at[2 + part],
        )

    for own in range(N_TM):

        @pl.when(t == own)
        def _():
            for hop in (2, 1, 3):
                for part in range(2):
                    share(part, (own + hop) % N_TM).start()

    for part in range(2):
        for side in range(2):
            halo(part, side).start()
    for own in range(N_TM):

        @pl.when(t == own)
        def _():
            for part in range(2):
                load(part, own).start()
            for part in range(2):
                load(part, own).wait()
                store(part, own).start()
            for part in range(2):
                store(part, own).wait()
            low, width, at = span(own)
            for part in range(2):
                for hop in (1, 3, 2):
                    g = (own + hop) % N_TM
                    pltpu.make_async_remote_copy(
                        src_ref=sources[part].at[:, pl.ds(low, width)],
                        dst_ref=out.at[pl.ds(g * ROWS + part * 64, 64), pl.ds(at, width)],
                        send_sem=send_sem.at[own, part],
                        recv_sem=recv_sem.at[g, part],
                        device_id=(s, own),
                        device_id_type=MESH,
                    ).wait_recv()
                    share(part, g).wait_send()
            if own in (0, N_TM - 1):
                at = 0 if own == 0 else WINDOW - HALO
                for part in range(2):
                    for g in range(N_TM):
                        pltpu.make_async_remote_copy(
                            src_ref=sources[part].at[:, pl.ds(0, HALO)],
                            dst_ref=out.at[pl.ds(g * ROWS + part * 64, 64), pl.ds(at, HALO)],
                            send_sem=halo_send.at[0, part],
                            recv_sem=halo_recv.at[g, part],
                            device_id=(s, own),
                            device_id_type=MESH,
                        ).wait_recv()

    for part in range(2):
        for side in range(2):
            halo(part, side).wait_send()


def exchange(prior, snaps):
    return pl.pallas_call(
        exchange_kernel,
        out_shape=jax.ShapeDtypeStruct((N_TM * ROWS, WINDOW), BF16),
        in_specs=[pl.BlockSpec(memory_space=pl.ANY)] * 2,
        out_specs=pl.BlockSpec(memory_space=pl.ANY),
        scratch_shapes=[
            pltpu.VMEM((ROWS, WINDOW), BF16),
            pltpu.SemaphoreType.DMA((N_TM, 2)),
            pltpu.SemaphoreType.DMA((N_TM, 2)),
            pltpu.SemaphoreType.DMA((2, 2)),
            pltpu.SemaphoreType.DMA((N_TM, 2)),
            pltpu.SemaphoreType.DMA((4,)),
        ],
        compiler_params=pltpu.CompilerParams(collective_id=0, has_side_effects=True),
        name="exchange",
    )(prior, snaps)


def pick_tile(nb, first, j, wide, width, factor, in_low):
    zero = jnp.zeros((BLOCK, 128), BF16)
    picks, pieces = [], []
    for k in range(NEIGHBOURS):
        low = nb[2 * j * NEIGHBOURS + k] - first
        high = nb[(2 * j + 1) * NEIGHBOURS + k] - first
        low_at = ((low + 1) >> 1) * 128 + (low & 1) * width
        high_at = (high >> 1) * 128 + (1 - (high & 1)) * width
        picks.append(
            jnp.where(
                in_low,
                wide[:, pl.ds(pl.multiple_of(low_at, 128), 128)],
                wide[:, pl.ds(pl.multiple_of(high_at, 128), 128)],
            )
        )
        block = factor[k, :, pl.ds(pl.multiple_of(j * 128, 128), 128)]
        pieces += [jnp.where(in_low, block, zero), jnp.where(in_low, zero, block)]
    return jnp.concatenate(picks, axis=1), jnp.concatenate(pieces, axis=0)


def weigh_kernel(place, nb, x, mass, w, gram, wide, factor, sem):
    s, t = place[0], place[1]
    fetch = pltpu.make_async_copy(
        mass.at[:, :, pl.ds(pl.multiple_of(t * SHARE, 128), SHARE)], factor, sem
    )
    fetch.start()
    first = s * LOCAL_BLOCKS + t * SHARE_BLOCKS - REACH
    in_low = lax.broadcasted_iota(jnp.int32, (1, 128), 1) < BLOCK
    wide[:, pl.ds(0, WINDOW)] = x[...]
    for m in range(TILES + 1):
        before = x[:, pl.ds(128 * max(m - 1, 0), 128)]
        after = x[:, pl.ds(128 * min(m, TILES - 1), 128)]
        wide[:, pl.ds(WINDOW + 128 * m, 128)] = jnp.concatenate(
            [before[:, BLOCK:], after[:, :BLOCK]], axis=1
        )
    fetch.wait()

    def one_tile(j, carry):
        modes, rows = pick_tile(nb, first, j, wide, WINDOW, factor, in_low)
        result = jnp.dot(modes, rows, preferred_element_type=F32)
        w[:, pl.ds(pl.multiple_of(j * 128, 128), 128)] = result.astype(BF16)
        return carry

    lax.fori_loop(0, SHARE_BLOCKS // 2, one_tile, 0, unroll=4)
    at = 0
    for a in range(N_TM):
        for b in range(a, N_TM):
            gram[at] = lax.dot_general(
                w[pl.ds(a * ROWS, ROWS), :],
                w[pl.ds(b * ROWS, ROWS), :],
                (((1,), (1,)), ((), ())),
                preferred_element_type=F32,
            )
            at += 1


def weigh(place, nb, x, mass):
    rows = N_TM * ROWS
    return pl.pallas_call(
        weigh_kernel,
        out_shape=(
            jax.ShapeDtypeStruct((rows, SHARE), BF16),
            jax.ShapeDtypeStruct((10, ROWS, ROWS), F32),
        ),
        in_specs=[
            pl.BlockSpec(memory_space=pltpu.SMEM),
            pl.BlockSpec(memory_space=pltpu.SMEM),
            pl.BlockSpec(memory_space=pltpu.VMEM),
            pl.BlockSpec(memory_space=pl.ANY),
        ],
        out_specs=(
            pl.BlockSpec(memory_space=pltpu.VMEM),
            pl.BlockSpec(memory_space=pltpu.VMEM),
        ),
        scratch_shapes=[
            pltpu.VMEM((rows, (2 * TILES + 1) * 128), BF16),
            pltpu.VMEM((NEIGHBOURS, BLOCK, SHARE), BF16),
            pltpu.SemaphoreType.DMA,
        ],
        name="weigh",
    )(place, nb, x, mass)


PIECE = 40


def reduce_kernel(inp, out, half, r_core, s_x, r_x, s_y, r_y, r_z, send_sem, recv_sem):
    s = lax.axis_index("space")
    x = lax.axis_index("tm")
    c = lax.rem(s, 2)
    y = lax.rem(s // 2, 4)
    z = s // 8

    def space_of(zz, yy, cc):
        return zz * 8 + yy * 2 + cc

    core_peer = (space_of(z, y, 1 - c), x)
    x_peers = [(s, lax.rem(x + d, 4)) for d in (1, 2, 3)]
    y_peers = [(space_of(z, lax.rem(y + d, 4), c), x) for d in (1, 2, 3)]
    z_peers = [(space_of(lax.rem(z + d, 8), y, c), x) for d in range(1, 8)]
    barrier = pltpu.get_barrier_semaphore()
    for peer in [core_peer] + x_peers + y_peers + z_peers:
        pl.semaphore_signal(barrier, inc=1, device_id=peer, device_id_type=MESH)
    pl.semaphore_wait(barrier, 14)

    def copy(src, dst, slot, peer):
        return pltpu.make_async_remote_copy(
            src_ref=src,
            dst_ref=dst,
            send_sem=send_sem.at[slot],
            recv_sem=recv_sem.at[slot],
            device_id=peer,
            device_id_type=MESH,
        )

    def run(copies):
        for one in copies:
            one.start()
        for one in copies:
            one.wait()

    run([copy(inp.at[1 - c], r_core, 0, core_peer)])
    half[...] = inp[c] + r_core[...]
    run(
        [
            copy(half.at[lax.rem(x + d, 4)], r_x.at[d - 1], d, x_peers[d - 1])
            for d in (2, 1, 3)
        ]
    )
    s_x[...] = half[x] + r_x[0] + r_x[1] + r_x[2]
    run(
        [
            copy(s_x.at[lax.rem(y + d, 4)], r_y.at[d - 1], 3 + d, y_peers[d - 1])
            for d in (2, 1, 3)
        ]
    )
    r_z[z] = s_x[y] + r_y[0] + r_y[1] + r_y[2]
    run([copy(r_z.at[z], r_z.at[z], 6 + d, z_peers[d - 1]) for d in (4, 3, 5, 2, 6, 1, 7)])
    total = r_z[0]
    for i in range(1, 8):
        total = total + r_z[i]
    out[c, x, y] = total
    run([copy(out.at[c, x, y], out.at[c, x, y], 13 + d, y_peers[d - 1]) for d in (2, 1, 3)])
    run([copy(out.at[c, x], out.at[c, x], 16 + d, x_peers[d - 1]) for d in (2, 1, 3)])
    run([copy(out.at[c], out.at[c], 20, core_peer)])


def all_reduce(gram):
    shape = (2, 4, 4, PIECE, 128)
    return pl.pallas_call(
        reduce_kernel,
        out_shape=jax.ShapeDtypeStruct(shape, F32),
        in_specs=[pl.BlockSpec(memory_space=pltpu.VMEM)],
        out_specs=pl.BlockSpec(memory_space=pltpu.VMEM),
        scratch_shapes=[
            pltpu.VMEM(shape[1:], F32),
            pltpu.VMEM(shape[1:], F32),
            pltpu.VMEM(shape[2:], F32),
            pltpu.VMEM((3,) + shape[2:], F32),
            pltpu.VMEM((1, PIECE, 128), F32),
            pltpu.VMEM((3, PIECE, 128), F32),
            pltpu.VMEM((8, PIECE, 128), F32),
            pltpu.SemaphoreType.DMA((21,)),
            pltpu.SemaphoreType.DMA((21,)),
        ],
        compiler_params=pltpu.CompilerParams(collective_id=1, has_side_effects=True),
        name="all_reduce",
    )(gram.reshape(shape)).reshape(10, ROWS, ROWS)


def eliminate(inners):
    sub = lax.broadcasted_iota(jnp.int32, (8, 128), 0)
    lane = lax.broadcasted_iota(jnp.int32, (8, 128), 1)
    grids = []
    for inner in inners:
        tiles = []
        for i in range(8):
            unit = jnp.where(lane == 8 * i + sub + BLOCK, 1.0, 0.0).astype(F32)
            left = jnp.concatenate([inner[8 * i : 8 * i + 8, :], jnp.zeros((8, BLOCK), F32)], axis=1)
            tiles.append(left + unit)
        grids.append(tiles)
    outs = [[] for _ in inners]
    for p in range(8):
        panels = [
            [[jnp.broadcast_to(tiles[i][:, 8 * p + q : 8 * p + q + 1], (8, 128)) for q in range(8)] for i in range(p, 8)]
            for tiles in grids
        ]
        roots = [jnp.ones((8, 128), F32) for _ in grids]
        for q in range(8):
            for m, (tiles, cols) in enumerate(zip(grids, panels)):
                pivot = jnp.broadcast_to(cols[0][q][q : q + 1, :], (8, 128))
                inv = 1.0 / pivot
                roots[m] = jnp.where(sub == q, pivot, roots[m])
                for r in range(q + 1, 8):
                    factor = jnp.broadcast_to(cols[0][r][q : q + 1, :], (8, 128)) * inv
                    for i in range(8 - p):
                        cols[i][r] = cols[i][r] - cols[i][q] * factor
                row = jnp.broadcast_to(tiles[p][q : q + 1, :], (8, 128)) * inv
                for i in range(p, 8):
                    change = cols[i - p][q] * row
                    if i == p:
                        change = jnp.where(sub > q, change, 0.0)
                    tiles[i] = tiles[i] - change
        for out, tiles, root in zip(outs, grids, roots):
            out.append(tiles[p] * lax.rsqrt(root))
    return [jnp.concatenate(out, axis=0) for out in outs]


def compress(grams):
    rows = [gram[:RANK, :] for gram in grams]
    products = rows
    zeros = jnp.zeros((BLOCK, ROWS), F32)

    def step(products):
        seconds = [dot_nn(p, g) for p, g in zip(products, grams)]
        inners = [dot_nt(p, q) for p, q in zip(products, seconds)]
        inverses = eliminate(inners)
        nexts = [
            dot_nn(inv, jnp.concatenate([zeros, q], axis=0)) for inv, q in zip(inverses, seconds)
        ]
        return inverses, nexts

    for _ in range(STEPS - 1):
        _, products = step(products)
    inverses, nexts = step(products)
    result = []
    for inv, p, q in zip(inverses, products, nexts):
        weights = dot_nn(inv, jnp.concatenate([zeros, p], axis=0))
        lengths = jnp.sqrt(jnp.sum(q * q, axis=1, keepdims=True) + 1e-06)
        result.append((weights * lengths).astype(BF16).astype(F32))
    return result


def merge_kernel(gram, out, full, below, middle, above):
    index = {}
    for a in range(N_TM):
        for b in range(a, N_TM):
            index[a, b] = len(index)
    for (a, b), at in index.items():
        block = gram[at]
        full[pl.ds(a * ROWS, ROWS), pl.ds(b * ROWS, ROWS)] = block
        if a != b:
            full[pl.ds(b * ROWS, ROWS), pl.ds(a * ROWS, ROWS)] = block.T
    below[...] = jnp.zeros_like(below)
    above[...] = jnp.zeros_like(above)
    lowest = compress([gram[index[g, g]] for g in range(N_TM)])
    for g in range(N_TM):
        below[pl.ds(g * RANK, RANK), pl.ds(g * ROWS, ROWS)] = lowest[g]
    for p in range(2):
        half = [
            dot_nn(lowest[g], full[pl.ds(g * ROWS, ROWS), pl.ds(2 * p * ROWS, 2 * ROWS)])
            for g in range(N_TM)
        ]
        middle[:, pl.ds(p * ROWS, ROWS)] = dot_nt(
            jnp.concatenate(half, axis=0),
            below[pl.ds(2 * p * RANK, 2 * RANK), pl.ds(2 * p * ROWS, 2 * ROWS)],
        )
    second = compress([middle[pl.ds(p * ROWS, ROWS), pl.ds(p * ROWS, ROWS)] for p in range(2)])
    for p in range(2):
        above[pl.ds(p * RANK, RANK), pl.ds(p * ROWS, ROWS)] = second[p]
    half = [dot_nn(second[p], middle[pl.ds(p * ROWS, ROWS), :]) for p in range(2)]
    last = compress([dot_nt(jnp.concatenate(half, axis=0), above[...])])[0]
    out[...] = dot_nn(dot_nn(last, above[...]), below[...]).astype(BF16)


def merge(gram):
    return pl.pallas_call(
        merge_kernel,
        out_shape=jax.ShapeDtypeStruct((RANK, N_TM * ROWS), BF16),
        in_specs=[pl.BlockSpec(memory_space=pltpu.VMEM)],
        out_specs=pl.BlockSpec(memory_space=pltpu.VMEM),
        scratch_shapes=[
            pltpu.VMEM((N_TM * ROWS, N_TM * ROWS), F32),
            pltpu.VMEM((N_TM * RANK, N_TM * ROWS), F32),
            pltpu.VMEM((N_TM * RANK, N_TM * RANK), F32),
            pltpu.VMEM((2 * RANK, 2 * ROWS), F32),
        ],
        name="merge",
    )(gram)


def shards(snapshots, prior_basis, mass_factor, neighbours):
    s = lax.axis_index("space")
    t = lax.axis_index("tm")
    place = jnp.stack([s, t]).astype(jnp.int32)
    nb = lax.dynamic_slice_in_dim(neighbours, t * SHARE_BLOCKS, SHARE_BLOCKS, 0).reshape(-1)
    x = exchange(prior_basis, snapshots)
    w, gram = weigh(place, nb, x, mass_factor)
    coefficients = merge(all_reduce(gram))
    own = lax.slice_in_dim(x, HALO, HALO + SHARE, axis=1)
    basis = jnp.dot(coefficients, own, preferred_element_type=F32).astype(BF16)
    weighted = jnp.dot(coefficients, w, preferred_element_type=F32).astype(BF16)
    return basis, weighted


def solution(mesh):
    return jax.shard_map(
        shards,
        mesh=mesh,
        in_specs=(P("tm", "space"), P("tm", "space"), P(None, None, "space"), P("space", None)),
        out_specs=(P(None, ("space", "tm")), P(None, ("space", "tm"))),
        check_vma=False,
    )
```

```python
import functools

import jax
import jax.numpy as jnp
from jax import lax
from jax.experimental import pallas as pl
from jax.experimental.pallas import tpu as pltpu
from jax.sharding import PartitionSpec as P

BLOCK = 64
RANK = 64
NEIGHBOURS = 7
REACH = 8
STEPS = 3
LOCAL_BLOCKS = 128
N_SPACE = 64
N_TM = 4
ROWS = 128
SLAB = LOCAL_BLOCKS * BLOCK
SHARE = SLAB // N_TM
HALO = REACH * BLOCK
WINDOW = SHARE + 2 * HALO
SHARE_BLOCKS = SHARE // BLOCK
TILES = WINDOW // 128
WIDE = SLAB + 2 * HALO
WIDE_TILES = WIDE // 128
HALO_TILES = HALO // 128
MESH = pl.DeviceIdType.MESH
HIGHEST = lax.Precision.HIGHEST
F32 = jnp.float32
BF16 = jnp.bfloat16


def dot_nn(a, b):
    return lax.dot_general(
        a, b, (((1,), (0,)), ((), ())), precision=HIGHEST, preferred_element_type=F32
    )


def dot_nt(a, b):
    return lax.dot_general(
        a, b, (((1,), (1,)), ((), ())), precision=HIGHEST, preferred_element_type=F32
    )


def eliminate(inners):
    sub = lax.broadcasted_iota(jnp.int32, (8, 128), 0)
    lane = lax.broadcasted_iota(jnp.int32, (8, 128), 1)
    grids = []
    for inner in inners:
        tiles = []
        for i in range(8):
            unit = jnp.where(lane == 8 * i + sub + BLOCK, 1.0, 0.0).astype(F32)
            left = jnp.concatenate([inner[8 * i : 8 * i + 8, :], jnp.zeros((8, BLOCK), F32)], axis=1)
            tiles.append(left + unit)
        grids.append(tiles)
    outs = [[] for _ in inners]
    for p in range(8):
        panels = [
            [[jnp.broadcast_to(tiles[i][:, 8 * p + q : 8 * p + q + 1], (8, 128)) for q in range(8)] for i in range(p, 8)]
            for tiles in grids
        ]
        roots = [jnp.ones((8, 128), F32) for _ in grids]
        for q in range(8):
            for m, (tiles, cols) in enumerate(zip(grids, panels)):
                pivot = jnp.broadcast_to(cols[0][q][q : q + 1, :], (8, 128))
                inv = 1.0 / pivot
                roots[m] = jnp.where(sub == q, pivot, roots[m])
                for r in range(q + 1, 8):
                    factor = jnp.broadcast_to(cols[0][r][q : q + 1, :], (8, 128)) * inv
                    for i in range(8 - p):
                        cols[i][r] = cols[i][r] - cols[i][q] * factor
                row = jnp.broadcast_to(tiles[p][q : q + 1, :], (8, 128)) * inv
                for i in range(p, 8):
                    change = cols[i - p][q] * row
                    if i == p:
                        change = jnp.where(sub > q, change, 0.0)
                    tiles[i] = tiles[i] - change
        for out, tiles, root in zip(outs, grids, roots):
            out.append(tiles[p] * lax.rsqrt(root))
    return [jnp.concatenate(out, axis=0) for out in outs]


def compress(grams):
    zeros = jnp.zeros((BLOCK, ROWS), F32)

    def apply(inverse, rows):
        return dot_nn(inverse, jnp.concatenate([zeros, rows], axis=0))

    def step(_, state):
        _, _, products = state
        seconds = [dot_nn(p, g) for p, g in zip(products, grams)]
        inverses = eliminate([dot_nt(p, q) for p, q in zip(products, seconds)])
        return inverses, products, [apply(inv, q) for inv, q in zip(inverses, seconds)]

    first = [gram[:RANK, :] for gram in grams]
    state = (first, first, first)
    for i in range(STEPS):
        state = step(i, state)
    inverses, products, nexts = state
    result = []
    for inv, p, q in zip(inverses, products, nexts):
        lengths = jnp.sqrt(jnp.sum(q * q, axis=1, keepdims=True) + 1e-06)
        result.append((apply(inv, p) * lengths).astype(BF16))
    return result


def tiles_of(neighbours, s):
    at = neighbours - (s * LOCAL_BLOCKS - REACH)
    second = lax.broadcasted_iota(jnp.int32, at.shape, 0) & 1
    moved = (at & 1) ^ second
    return ((at + 1 - second) >> 1) + moved * WIDE_TILES


def pick_modes(tile, j, tiles, in_low):
    picks = []
    for k in range(NEIGHBOURS):
        low = tiles[tile[2 * j, k]]
        high = tiles[tile[2 * j + 1, k]]
        picks.append(jnp.where(in_low, low, high))
    return jnp.concatenate(picks, axis=1)


def pick_factor(j, factor, in_low):
    zero = jnp.zeros((BLOCK, 128), BF16)
    pieces = []
    for k in range(NEIGHBOURS):
        block = factor[k, :, pl.ds(pl.multiple_of(j * 128, 128), 128)]
        pieces += [jnp.where(in_low, block, zero), jnp.where(in_low, zero, block)]
    return jnp.concatenate(pieces, axis=0)


def halves(before, after):
    return jnp.concatenate([before[:, BLOCK:], after[:, :BLOCK]], axis=1)


def widen(wide, tiles, low, high, unroll):
    def one_tile(m, carry):
        before = wide[:, pl.ds(pl.multiple_of(128 * (m - 1), 128), 128)]
        after = wide[:, pl.ds(pl.multiple_of(128 * m, 128), 128)]
        tiles[m] = after
        tiles[WIDE_TILES + m] = halves(before, after)
        return carry

    lax.fori_loop(low, high, one_tile, 0, unroll=unroll)


def widen_ends(wide, tiles):
    last = wide.shape[1] // 128 - 1
    first = wide[:, pl.ds(0, 128)]
    tiles[0] = first
    tiles[WIDE_TILES] = halves(first, first)
    end = wide[:, pl.ds(128 * last, 128)]
    tiles[WIDE_TILES + last + 1] = halves(end, end)


def lowest_kernel(
    tile,
    prior,
    snaps,
    mass,
    rows_out,
    weighted_out,
    gram_out,
    own,
    own_tiles,
    weights_own,
    weights_in,
    factor,
    gram,
    r_plane,
    r_z,
    total,
    coefs,
    send_sem,
    recv_sem,
    local_sem,
    sum_send,
    sum_recv,
):
    s = lax.axis_index("space")
    t = lax.axis_index("tm")
    c = lax.rem(s, 2)
    y = lax.rem(s // 2, 4)
    z = s // 8
    up = lax.rem(s + 1, N_SPACE)
    down = lax.rem(s + N_SPACE - 1, N_SPACE)
    sources = (prior, snaps)
    chunk = SLAB // 4

    def half(part):
        return pl.ds(part * 64, 64)

    loads = [
        pltpu.make_async_copy(
            sources[part], own.at[half(part), pl.ds(HALO, SLAB)], local_sem.at[part]
        )
        for part in range(2)
    ]
    fetches = [
        pltpu.make_async_copy(
            mass.at[:, :, pl.ds(chunk * i, chunk)],
            factor.at[:, :, pl.ds(chunk * i, chunk)],
            local_sem.at[2 + i],
        )
        for i in range(4)
    ]
    for one in loads + fetches:
        one.start()

    def space_of(zz, yy, cc):
        return zz * 8 + yy * 2 + cc

    x_peers = [(s, lax.rem(t + h, 4)) for h in (1, 2, 3)]
    me = c * 4 + y
    plane = []
    for dc, dy in ((1, 2), (0, 2), (1, 1), (1, 3), (0, 1), (0, 3), (1, 0)):
        pc, py = lax.rem(c + dc, 2), lax.rem(y + dy, 4)
        plane.append((pc * 4 + py, (space_of(z, py, pc), t)))
    z_peers = [(space_of(lax.rem(z + d, 8), y, c), t) for d in range(1, 8)]

    barrier = pltpu.get_barrier_semaphore()
    for peer in x_peers + [where for _, where in plane] + z_peers + [(up, t), (down, t)]:
        pl.semaphore_signal(barrier, inc=1, device_id=peer, device_id_type=MESH)

    pl.semaphore_wait(barrier, 19)

    def remote(src, dst, slot, peer, part):
        return pltpu.make_async_remote_copy(
            src_ref=src,
            dst_ref=dst,
            send_sem=send_sem.at[slot, part],
            recv_sem=recv_sem.at[slot, part],
            device_id=peer,
            device_id_type=MESH,
        )

    def share(hop):
        return remote(
            weights_own.at[:, pl.ds(pl.multiple_of(lax.rem(t + hop, 4) * SHARE, 128), SHARE)],
            weights_in.at[hop - 1],
            hop - 1,
            x_peers[hop - 1],
            0,
        )

    def own_edge(part, side):
        low, at = (SLAB - HALO, 0) if side == 0 else (0, WIDE - HALO)
        return remote(
            sources[part].at[:, pl.ds(low, HALO)],
            own.at[half(part), pl.ds(at, HALO)],
            3 + side,
            (up, t) if side == 0 else (down, t),
            part,
        )

    for part in range(2):
        for side in range(2):
            own_edge(part, side).start()

    in_low = lax.broadcasted_iota(jnp.int32, (1, 128), 1) < BLOCK
    for one in loads:
        one.wait()
    widen(own, own_tiles, HALO_TILES + 1, WIDE_TILES - HALO_TILES, 9)
    for part in range(2):
        for side in range(2):
            own_edge(part, side).wait()
    widen(own, own_tiles, 1, HALO_TILES + 1, HALO_TILES)
    widen(own, own_tiles, WIDE_TILES - HALO_TILES, WIDE_TILES, HALO_TILES)
    widen_ends(own, own_tiles)
    for one in fetches:
        one.wait()

    def own_quarter(quarter):
        def own_tile(i, carry):
            j = quarter * (SHARE_BLOCKS // 2) + i
            modes = pick_modes(tile, j, own_tiles, in_low)
            result = jnp.dot(modes, pick_factor(j, factor, in_low), preferred_element_type=F32)
            weights_own[:, pl.ds(pl.multiple_of(j * 128, 128), 128)] = result.astype(BF16)
            return carry

        lax.fori_loop(0, SHARE_BLOCKS // 2, own_tile, 0, unroll=4)

    for hop in (2, 1, 3):
        own_quarter(lax.rem(t + hop, 4))
        share(hop).start()
    own_quarter(t)
    local = lax.dot_general(
        weights_own[...], weights_own[...], (((1,), (1,)), ((), ())), preferred_element_type=F32
    )
    for i in range(8):
        gram[i] = local[16 * i : 16 * i + 16, :]

    def over(src, dst, slot, peer):
        return pltpu.make_async_remote_copy(
            src_ref=src,
            dst_ref=dst,
            send_sem=sum_send.at[slot],
            recv_sem=sum_recv.at[slot],
            device_id=peer,
            device_id_type=MESH,
        )

    def run(copies):
        for one in copies:
            one.start()
        for one in copies:
            one.wait()

    run([over(gram.at[owner], r_plane.at[i], i, where) for i, (owner, where) in enumerate(plane)])
    piece = gram[me]
    for i in range(7):
        piece = piece + r_plane[i]
    r_z[z] = piece
    run([over(r_z.at[z], r_z.at[z], 6 + d, z_peers[d - 1]) for d in (4, 3, 5, 2, 6, 1, 7)])
    piece = r_z[0]
    for i in range(1, 8):
        piece = piece + r_z[i]
    total[me] = piece
    run([over(total.at[me], total.at[me], 14 + i, where) for i, (_, where) in enumerate(plane)])

    summed = jnp.concatenate([total[i] for i in range(8)], axis=0)
    coefs[t] = compress([summed])[0]
    passed = [remote(coefs.at[t], coefs.at[t], 4 + h, x_peers[h - 1], 0) for h in (2, 1, 3)]
    for one in passed:
        one.start()

    rows_out[...] = jnp.dot(
        coefs[t], own[:, pl.ds(HALO, SLAB)], preferred_element_type=F32
    ).astype(BF16)
    for hop in (1, 3, 2):
        share(hop).wait()

    def put(group, weighted):
        weighted_out[pl.ds(pl.multiple_of(group * RANK, RANK), RANK), :] = jnp.dot(
            coefs[group], weighted, preferred_element_type=F32
        ).astype(BF16)

    put(t, weights_own[:, pl.ds(pl.multiple_of(t * SHARE, 128), SHARE)])
    for one in passed:
        one.wait()
    for hop in (1, 2, 3):
        put(lax.rem(t + N_TM - hop, N_TM), weights_in[hop - 1])
    for a in range(2):
        for b in range(2):
            gram_out[2 * a + b] = lax.dot_general(
                weighted_out[pl.ds(a * ROWS, ROWS), :],
                weighted_out[pl.ds(b * ROWS, ROWS), :],
                (((1,), (1,)), ((), ())),
                preferred_element_type=F32,
            )


def lowest(tile, prior, snaps, mass):
    piece = (16, 128)
    vmem = pl.BlockSpec(memory_space=pltpu.VMEM)
    anywhere = pl.BlockSpec(memory_space=pl.ANY)
    return pl.pallas_call(
        lowest_kernel,
        out_shape=(
            jax.ShapeDtypeStruct((RANK, SLAB), BF16),
            jax.ShapeDtypeStruct((N_TM * RANK, SHARE), BF16),
            jax.ShapeDtypeStruct((4, ROWS, ROWS), F32),
        ),
        in_specs=[pl.BlockSpec(memory_space=pltpu.SMEM), anywhere, anywhere, anywhere],
        out_specs=(vmem, vmem, vmem),
        scratch_shapes=[
            pltpu.VMEM((ROWS, WIDE), BF16),
            pltpu.VMEM((2 * WIDE_TILES + 1, ROWS, 128), BF16),
            pltpu.VMEM((ROWS, SLAB), BF16),
            pltpu.VMEM((3, ROWS, SHARE), BF16),
            pltpu.VMEM((NEIGHBOURS, BLOCK, SLAB), BF16),
            pltpu.VMEM((8,) + piece, F32),
            pltpu.VMEM((7,) + piece, F32),
            pltpu.VMEM((8,) + piece, F32),
            pltpu.VMEM((8,) + piece, F32),
            pltpu.VMEM((N_TM, RANK, ROWS), BF16),
            pltpu.SemaphoreType.DMA((8, 2)),
            pltpu.SemaphoreType.DMA((8, 2)),
            pltpu.SemaphoreType.DMA((6,)),
            pltpu.SemaphoreType.DMA((21,)),
            pltpu.SemaphoreType.DMA((21,)),
        ],
        compiler_params=pltpu.CompilerParams(collective_id=0, has_side_effects=True),
        name="lowest",
    )(tile, prior, snaps, mass)


PIECE = 16


def reduce_kernel(
    inp,
    rows,
    out,
    rows_out,
    r_plane,
    r_z,
    plane_send,
    plane_recv,
    z_send,
    z_recv,
    rows_send,
    rows_recv,
):
    s = lax.axis_index("space")
    x = lax.axis_index("tm")
    c = lax.rem(s, 2)
    y = lax.rem(s // 2, 4)
    z = s // 8
    me = c * 16 + x * 4 + y
    hops = [(dc, dx, dy) for dx in (2, 1, 3, 0) for dy in (2, 1, 3, 0) for dc in (1, 0)]
    plane = []
    for dc, dx, dy in hops[:-1]:
        pc, px, py = lax.rem(c + dc, 2), lax.rem(x + dx, 4), lax.rem(y + dy, 4)
        plane.append((pc * 16 + px * 4 + py, (z * 8 + py * 2 + pc, px)))
    z_peers = [(lax.rem(z + d, 8) * 8 + y * 2 + c, x) for d in range(1, 8)]
    barrier = pltpu.get_barrier_semaphore()
    for peer in [where for _, where in plane] + z_peers:
        pl.semaphore_signal(barrier, inc=1, device_id=peer, device_id_type=MESH)
    pl.semaphore_wait(barrier, 38)

    def copy(src, dst, send, recv, slot, peer):
        return pltpu.make_async_remote_copy(
            src_ref=src,
            dst_ref=dst,
            send_sem=send.at[slot],
            recv_sem=recv.at[slot],
            device_id=peer,
            device_id_type=MESH,
        )

    def run(copies):
        for one in copies:
            one.start()
        for one in copies:
            one.wait()

    run(
        [
            copy(inp.at[owner], r_plane.at[i], plane_send, plane_recv, i, where)
            for i, (owner, where) in enumerate(plane)
        ]
    )
    own_rows = pl.ds(pl.multiple_of(x * RANK, RANK), RANK)

    def columns(member):
        return pl.ds(pl.multiple_of(member * SHARE, 128), SHARE)

    moved = [
        copy(
            rows.at[:, columns(lax.rem(x + hop, 4))],
            rows_out.at[own_rows, :],
            rows_send,
            rows_recv,
            hop - 1,
            (s, lax.rem(x + hop, 4)),
        )
        for hop in (2, 1, 3)
    ]
    piece = inp[me]
    for i in range(31):
        piece = piece + r_plane[i]
    r_z[z] = piece
    around = [
        copy(r_z.at[z], r_z.at[z], z_send, z_recv, d - 1, z_peers[d - 1])
        for d in (4, 3, 5, 2, 6, 1, 7)
    ]
    for one in around + moved:
        one.start()
    rows_out[own_rows, :] = rows[:, columns(x)]
    for one in around:
        one.wait()
    piece = r_z[0]
    for i in range(1, 8):
        piece = piece + r_z[i]
    out[me] = piece
    run(
        [
            copy(out.at[me], out.at[me], plane_send, plane_recv, 31 + i, where)
            for i, (_, where) in enumerate(plane)
        ]
    )
    for one in moved:
        one.wait()


def all_reduce(gram, rows):
    shape = (32, PIECE, 128)
    vmem = pl.BlockSpec(memory_space=pltpu.VMEM)
    total, gathered = pl.pallas_call(
        reduce_kernel,
        out_shape=(
            jax.ShapeDtypeStruct(shape, F32),
            jax.ShapeDtypeStruct((N_TM * RANK, SHARE), BF16),
        ),
        in_specs=[vmem, vmem],
        out_specs=(vmem, vmem),
        scratch_shapes=[
            pltpu.VMEM((31, PIECE, 128), F32),
            pltpu.VMEM((8, PIECE, 128), F32),
            pltpu.SemaphoreType.DMA((62,)),
            pltpu.SemaphoreType.DMA((62,)),
            pltpu.SemaphoreType.DMA((7,)),
            pltpu.SemaphoreType.DMA((7,)),
            pltpu.SemaphoreType.DMA((3,)),
            pltpu.SemaphoreType.DMA((3,)),
        ],
        compiler_params=pltpu.CompilerParams(collective_id=1, has_side_effects=True),
        name="all_reduce",
    )(gram.reshape(shape), rows)
    return total.reshape(4, ROWS, ROWS), gathered


def merge_kernel(gram, rows, weighted, rows_out, weighted_out, above):
    above[...] = jnp.zeros_like(above)
    second = [c.astype(F32) for c in compress([gram[0], gram[3]])]
    for p in range(2):
        above[pl.ds(p * RANK, RANK), pl.ds(p * ROWS, ROWS)] = second[p]
    mixed = [
        jnp.concatenate([dot_nn(second[p], gram[2 * p + q]) for q in range(2)], axis=1)
        for p in range(2)
    ]
    last = compress([dot_nt(jnp.concatenate(mixed, axis=0), above[...])])[0]
    mix = dot_nn(last.astype(F32), above[...]).astype(BF16)
    rows_out[...] = jnp.dot(mix, rows[...], preferred_element_type=F32).astype(BF16)
    weighted_out[...] = jnp.dot(mix, weighted[...], preferred_element_type=F32).astype(BF16)


def merge(gram, rows, weighted):
    vmem = pl.BlockSpec(memory_space=pltpu.VMEM)
    return pl.pallas_call(
        merge_kernel,
        out_shape=(jax.ShapeDtypeStruct((RANK, SHARE), BF16),) * 2,
        in_specs=[vmem] * 3,
        out_specs=(vmem, vmem),
        scratch_shapes=[pltpu.VMEM((2 * RANK, 2 * ROWS), F32)],
        name="merge",
    )(gram, rows, weighted)


def shards(snapshots, prior_basis, mass_factor, neighbours):
    tile = tiles_of(neighbours, lax.axis_index("space"))
    rows, weighted, gram = lowest(tile, prior_basis, snapshots, mass_factor)
    return merge(*all_reduce(gram, rows), weighted)


def solution(mesh):
    return jax.shard_map(
        shards,
        mesh=mesh,
        in_specs=(P("tm", "space"), P("tm", "space"), P(None, None, "space"), P("space", None)),
        out_specs=(P(None, ("space", "tm")), P(None, ("space", "tm"))),
        check_vma=False,
    )
```

```python
import functools

import jax
import jax.numpy as jnp
from jax import lax
from jax.experimental import pallas as pl
from jax.experimental.pallas import tpu as pltpu
from jax.sharding import PartitionSpec as P

BLOCK = 64
RANK = 64
NEIGHBOURS = 7
REACH = 8
STEPS = 3
LOCAL_BLOCKS = 128
N_SPACE = 64
N_TM = 4
ROWS = 128
SLAB = LOCAL_BLOCKS * BLOCK
SHARE = SLAB // N_TM
HALO = REACH * BLOCK
WINDOW = SHARE + 2 * HALO
SHARE_BLOCKS = SHARE // BLOCK
TILES = WINDOW // 128
WIDE = SLAB + 2 * HALO
WIDE_TILES = WIDE // 128
HALO_TILES = HALO // 128
MESH = pl.DeviceIdType.MESH
HIGHEST = lax.Precision.HIGHEST
F32 = jnp.float32
BF16 = jnp.bfloat16


def dot_nn(a, b):
    return lax.dot_general(
        a, b, (((1,), (0,)), ((), ())), precision=HIGHEST, preferred_element_type=F32
    )


def dot_nt(a, b):
    return lax.dot_general(
        a, b, (((1,), (1,)), ((), ())), precision=HIGHEST, preferred_element_type=F32
    )


def eliminate(inners):
    sub = lax.broadcasted_iota(jnp.int32, (8, 128), 0)
    lane = lax.broadcasted_iota(jnp.int32, (8, 128), 1)
    grids = []
    for inner in inners:
        tiles = []
        for i in range(8):
            unit = jnp.where(lane == 8 * i + sub + BLOCK, 1.0, 0.0).astype(F32)
            left = jnp.concatenate([inner[8 * i : 8 * i + 8, :], jnp.zeros((8, BLOCK), F32)], axis=1)
            tiles.append(left + unit)
        grids.append(tiles)
    outs = [[] for _ in inners]
    for p in range(8):
        panels = [
            [[jnp.broadcast_to(tiles[i][:, 8 * p + q : 8 * p + q + 1], (8, 128)) for q in range(8)] for i in range(p, 8)]
            for tiles in grids
        ]
        roots = [jnp.ones((8, 128), F32) for _ in grids]
        for q in range(8):
            for m, (tiles, cols) in enumerate(zip(grids, panels)):
                pivot = jnp.broadcast_to(cols[0][q][q : q + 1, :], (8, 128))
                inv = 1.0 / pivot
                roots[m] = jnp.where(sub == q, pivot, roots[m])
                for r in range(q + 1, 8):
                    factor = jnp.broadcast_to(cols[0][r][q : q + 1, :], (8, 128)) * inv
                    for i in range(8 - p):
                        cols[i][r] = cols[i][r] - cols[i][q] * factor
                row = jnp.broadcast_to(tiles[p][q : q + 1, :], (8, 128)) * inv
                for i in range(p, 8):
                    change = cols[i - p][q] * row
                    if i == p:
                        change = jnp.where(sub > q, change, 0.0)
                    tiles[i] = tiles[i] - change
        for out, tiles, root in zip(outs, grids, roots):
            out.append(tiles[p] * lax.rsqrt(root))
    return [jnp.concatenate(out, axis=0) for out in outs]


def compress(grams):
    zeros = jnp.zeros((BLOCK, ROWS), F32)

    def apply(inverse, rows):
        return dot_nn(inverse, jnp.concatenate([zeros, rows], axis=0))

    def step(_, state):
        _, _, products = state
        seconds = [dot_nn(p, g) for p, g in zip(products, grams)]
        inverses = eliminate([dot_nt(p, q) for p, q in zip(products, seconds)])
        return inverses, products, [apply(inv, q) for inv, q in zip(inverses, seconds)]

    first = [gram[:RANK, :] for gram in grams]
    state = (first, first, first)
    for i in range(STEPS):
        state = step(i, state)
    inverses, products, nexts = state
    result = []
    for inv, p, q in zip(inverses, products, nexts):
        lengths = jnp.sqrt(jnp.sum(q * q, axis=1, keepdims=True) + 1e-06)
        result.append((apply(inv, p) * lengths).astype(BF16))
    return result


def tiles_of(neighbours, s):
    at = neighbours - (s * LOCAL_BLOCKS - REACH)
    second = lax.broadcasted_iota(jnp.int32, at.shape, 0) & 1
    moved = (at & 1) ^ second
    return ((at + 1 - second) >> 1) + moved * WIDE_TILES


def pick_modes(tile, j, tiles, in_low):
    picks = []
    for k in range(NEIGHBOURS):
        low = tiles[tile[2 * j, k]]
        high = tiles[tile[2 * j + 1, k]]
        picks.append(jnp.where(in_low, low, high))
    return jnp.concatenate(picks, axis=1)


def pick_factor(j, factor, in_low):
    zero = jnp.zeros((BLOCK, 128), BF16)
    pieces = []
    for k in range(NEIGHBOURS):
        block = factor[k, :, pl.ds(pl.multiple_of(j * 128, 128), 128)]
        pieces += [jnp.where(in_low, block, zero), jnp.where(in_low, zero, block)]
    return jnp.concatenate(pieces, axis=0)


def halves(before, after):
    return jnp.concatenate([before[:, BLOCK:], after[:, :BLOCK]], axis=1)


def widen(wide, tiles, low, high, unroll):
    def one_tile(m, carry):
        before = wide[:, pl.ds(pl.multiple_of(128 * (m - 1), 128), 128)]
        after = wide[:, pl.ds(pl.multiple_of(128 * m, 128), 128)]
        tiles[m] = after
        tiles[WIDE_TILES + m] = halves(before, after)
        return carry

    lax.fori_loop(low, high, one_tile, 0, unroll=unroll)


def widen_ends(wide, tiles):
    last = wide.shape[1] // 128 - 1
    first = wide[:, pl.ds(0, 128)]
    tiles[0] = first
    tiles[WIDE_TILES] = halves(first, first)
    end = wide[:, pl.ds(128 * last, 128)]
    tiles[WIDE_TILES + last + 1] = halves(end, end)


def lowest_kernel(
    tile,
    prior,
    snaps,
    mass,
    rows_out,
    weighted_out,
    gram_out,
    own,
    own_tiles,
    weights_own,
    weights_in,
    factor,
    gram,
    r_plane,
    r_z,
    total,
    coefs,
    send_sem,
    recv_sem,
    local_sem,
    sum_send,
    sum_recv,
):
    s = lax.axis_index("space")
    t = lax.axis_index("tm")
    c = lax.rem(s, 2)
    y = lax.rem(s // 2, 4)
    z = s // 8
    up = lax.rem(s + 1, N_SPACE)
    down = lax.rem(s + N_SPACE - 1, N_SPACE)
    sources = (prior, snaps)
    chunk = SLAB // 4

    def half(part):
        return pl.ds(part * 64, 64)

    loads = [
        pltpu.make_async_copy(
            sources[part], own.at[half(part), pl.ds(HALO, SLAB)], local_sem.at[part]
        )
        for part in range(2)
    ]
    fetches = [
        pltpu.make_async_copy(
            mass.at[:, :, pl.ds(chunk * i, chunk)],
            factor.at[:, :, pl.ds(chunk * i, chunk)],
            local_sem.at[2 + i],
        )
        for i in range(4)
    ]
    for one in loads + fetches:
        one.start()

    def space_of(zz, yy, cc):
        return zz * 8 + yy * 2 + cc

    x_peers = [(s, lax.rem(t + h, 4)) for h in (1, 2, 3)]
    me = c * 4 + y
    plane = []
    for dc, dy in ((1, 2), (0, 2), (1, 1), (1, 3), (0, 1), (0, 3), (1, 0)):
        pc, py = lax.rem(c + dc, 2), lax.rem(y + dy, 4)
        plane.append((pc * 4 + py, (space_of(z, py, pc), t)))
    z_peers = [(space_of(lax.rem(z + d, 8), y, c), t) for d in range(1, 8)]

    barrier = pltpu.get_barrier_semaphore()
    for peer in x_peers + [where for _, where in plane] + z_peers + [(up, t), (down, t)]:
        pl.semaphore_signal(barrier, inc=1, device_id=peer, device_id_type=MESH)

    pl.semaphore_wait(barrier, 19)

    def remote(src, dst, slot, peer, part):
        return pltpu.make_async_remote_copy(
            src_ref=src,
            dst_ref=dst,
            send_sem=send_sem.at[slot, part],
            recv_sem=recv_sem.at[slot, part],
            device_id=peer,
            device_id_type=MESH,
        )

    def share(hop):
        return remote(
            weights_own.at[:, pl.ds(pl.multiple_of(lax.rem(t + hop, 4) * SHARE, 128), SHARE)],
            weights_in.at[hop - 1],
            hop - 1,
            x_peers[hop - 1],
            0,
        )

    def own_edge(part, side):
        low, at = (SLAB - HALO, 0) if side == 0 else (0, WIDE - HALO)
        return remote(
            sources[part].at[:, pl.ds(low, HALO)],
            own.at[half(part), pl.ds(at, HALO)],
            3 + side,
            (up, t) if side == 0 else (down, t),
            part,
        )

    for part in range(2):
        for side in range(2):
            own_edge(part, side).start()

    in_low = lax.broadcasted_iota(jnp.int32, (1, 128), 1) < BLOCK
    for one in loads:
        one.wait()
    widen(own, own_tiles, HALO_TILES + 1, WIDE_TILES - HALO_TILES, 9)
    for part in range(2):
        for side in range(2):
            own_edge(part, side).wait()
    widen(own, own_tiles, 1, HALO_TILES + 1, HALO_TILES)
    widen(own, own_tiles, WIDE_TILES - HALO_TILES, WIDE_TILES, HALO_TILES)
    widen_ends(own, own_tiles)
    for one in fetches:
        one.wait()

    def own_quarter(quarter):
        def own_tile(i, carry):
            j = quarter * (SHARE_BLOCKS // 2) + i
            modes = pick_modes(tile, j, own_tiles, in_low)
            result = jnp.dot(modes, pick_factor(j, factor, in_low), preferred_element_type=F32)
            weights_own[:, pl.ds(pl.multiple_of(j * 128, 128), 128)] = result.astype(BF16)
            return carry

        lax.fori_loop(0, SHARE_BLOCKS // 2, own_tile, 0, unroll=4)

    for hop in (2, 1, 3):
        own_quarter(lax.rem(t + hop, 4))
        share(hop).start()
    own_quarter(t)
    local = lax.dot_general(
        weights_own[...], weights_own[...], (((1,), (1,)), ((), ())), preferred_element_type=F32
    )
    for i in range(8):
        gram[i] = local[16 * i : 16 * i + 16, :]

    def over(src, dst, slot, peer):
        return pltpu.make_async_remote_copy(
            src_ref=src,
            dst_ref=dst,
            send_sem=sum_send.at[slot],
            recv_sem=sum_recv.at[slot],
            device_id=peer,
            device_id_type=MESH,
        )

    def run(copies):
        for one in copies:
            one.start()
        for one in copies:
            one.wait()

    run([over(gram.at[owner], r_plane.at[i], i, where) for i, (owner, where) in enumerate(plane)])
    piece = gram[me]
    for i in range(7):
        piece = piece + r_plane[i]
    r_z[z] = piece
    run([over(r_z.at[z], r_z.at[z], 6 + d, z_peers[d - 1]) for d in (4, 3, 5, 2, 6, 1, 7)])
    piece = r_z[0]
    for i in range(1, 8):
        piece = piece + r_z[i]
    total[me] = piece
    run([over(total.at[me], total.at[me], 14 + i, where) for i, (_, where) in enumerate(plane)])

    summed = jnp.concatenate([total[i] for i in range(8)], axis=0)
    coefs[t] = compress([summed])[0]
    passed = [remote(coefs.at[t], coefs.at[t], 4 + h, x_peers[h - 1], 0) for h in (2, 1, 3)]
    for one in passed:
        one.start()

    rows_out[...] = jnp.dot(
        coefs[t], own[:, pl.ds(HALO, SLAB)], preferred_element_type=F32
    ).astype(BF16)
    for hop in (1, 3, 2):
        share(hop).wait()

    def put(group, weighted):
        weighted_out[pl.ds(pl.multiple_of(group * RANK, RANK), RANK), :] = jnp.dot(
            coefs[group], weighted, preferred_element_type=F32
        ).astype(BF16)

    put(t, weights_own[:, pl.ds(pl.multiple_of(t * SHARE, 128), SHARE)])
    for one in passed:
        one.wait()
    for hop in (1, 2, 3):
        put(lax.rem(t + N_TM - hop, N_TM), weights_in[hop - 1])
    for a in range(2):
        for b in range(2):
            gram_out[2 * a + b] = lax.dot_general(
                weighted_out[pl.ds(a * ROWS, ROWS), :],
                weighted_out[pl.ds(b * ROWS, ROWS), :],
                (((1,), (1,)), ((), ())),
                preferred_element_type=F32,
            )


def lowest(tile, prior, snaps, mass):
    piece = (16, 128)
    vmem = pl.BlockSpec(memory_space=pltpu.VMEM)
    anywhere = pl.BlockSpec(memory_space=pl.ANY)
    return pl.pallas_call(
        lowest_kernel,
        out_shape=(
            jax.ShapeDtypeStruct((RANK, SLAB), BF16),
            jax.ShapeDtypeStruct((N_TM * RANK, SHARE), BF16),
            jax.ShapeDtypeStruct((4, ROWS, ROWS), F32),
        ),
        in_specs=[pl.BlockSpec(memory_space=pltpu.SMEM), anywhere, anywhere, anywhere],
        out_specs=(vmem, vmem, vmem),
        scratch_shapes=[
            pltpu.VMEM((ROWS, WIDE), BF16),
            pltpu.VMEM((2 * WIDE_TILES + 1, ROWS, 128), BF16),
            pltpu.VMEM((ROWS, SLAB), BF16),
            pltpu.VMEM((3, ROWS, SHARE), BF16),
            pltpu.VMEM((NEIGHBOURS, BLOCK, SLAB), BF16),
            pltpu.VMEM((8,) + piece, F32),
            pltpu.VMEM((7,) + piece, F32),
            pltpu.VMEM((8,) + piece, F32),
            pltpu.VMEM((8,) + piece, F32),
            pltpu.VMEM((N_TM, RANK, ROWS), BF16),
            pltpu.SemaphoreType.DMA((8, 2)),
            pltpu.SemaphoreType.DMA((8, 2)),
            pltpu.SemaphoreType.DMA((6,)),
            pltpu.SemaphoreType.DMA((21,)),
            pltpu.SemaphoreType.DMA((21,)),
        ],
        compiler_params=pltpu.CompilerParams(collective_id=0, has_side_effects=True),
        name="lowest",
    )(tile, prior, snaps, mass)


PIECE = 16


def merge_kernel(
    inp,
    rows,
    weighted,
    rows_out,
    weighted_out,
    out,
    rows_in,
    weighted_in,
    above,
    r_plane,
    r_z,
    plane_send,
    plane_recv,
    z_send,
    z_recv,
    rows_send,
    rows_recv,
    local_sem,
):
    s = lax.axis_index("space")
    x = lax.axis_index("tm")
    c = lax.rem(s, 2)
    y = lax.rem(s // 2, 4)
    z = s // 8
    me = c * 16 + x * 4 + y
    hops = [(dc, dx, dy) for dx in (2, 1, 3, 0) for dy in (2, 1, 3, 0) for dc in (1, 0)]
    plane = []
    for dc, dx, dy in hops[:-1]:
        pc, px, py = lax.rem(c + dc, 2), lax.rem(x + dx, 4), lax.rem(y + dy, 4)
        plane.append((pc * 16 + px * 4 + py, (z * 8 + py * 2 + pc, px)))
    z_peers = [(lax.rem(z + d, 8) * 8 + y * 2 + c, x) for d in range(1, 8)]
    own_rows = pl.ds(pl.multiple_of(x * RANK, RANK), RANK)

    def columns(member):
        return pl.ds(pl.multiple_of(member * SHARE, 128), SHARE)

    fetched = [
        pltpu.make_async_copy(weighted, weighted_in, local_sem.at[0]),
        pltpu.make_async_copy(rows.at[:, columns(x)], rows_in.at[own_rows, :], local_sem.at[1]),
    ]
    for one in fetched:
        one.start()
    barrier = pltpu.get_barrier_semaphore()
    for peer in [where for _, where in plane] + z_peers:
        pl.semaphore_signal(barrier, inc=1, device_id=peer, device_id_type=MESH)
    pl.semaphore_wait(barrier, 38)

    def copy(src, dst, send, recv, slot, peer):
        return pltpu.make_async_remote_copy(
            src_ref=src,
            dst_ref=dst,
            send_sem=send.at[slot],
            recv_sem=recv.at[slot],
            device_id=peer,
            device_id_type=MESH,
        )

    def run(copies):
        for one in copies:
            one.start()
        for one in copies:
            one.wait()

    run(
        [
            copy(inp.at[owner], r_plane.at[i], plane_send, plane_recv, i, where)
            for i, (owner, where) in enumerate(plane)
        ]
    )
    piece = inp[me]
    for i in range(31):
        piece = piece + r_plane[i]
    r_z[z] = piece
    run(
        [
            copy(r_z.at[z], r_z.at[z], z_send, z_recv, d - 1, z_peers[d - 1])
            for d in (4, 3, 5, 2, 6, 1, 7)
        ]
    )
    piece = r_z[0]
    for i in range(1, 8):
        piece = piece + r_z[i]
    out[me] = piece
    run(
        [
            copy(out.at[me], out.at[me], plane_send, plane_recv, 31 + i, where)
            for i, (_, where) in enumerate(plane)
        ]
    )

    moved = [
        copy(
            rows.at[:, columns(lax.rem(x + hop, 4))],
            rows_in.at[own_rows, :],
            rows_send,
            rows_recv,
            hop - 1,
            (s, lax.rem(x + hop, 4)),
        )
        for hop in (2, 1, 3)
    ]
    for one in moved:
        one.start()

    above[...] = jnp.zeros_like(above)
    gram = [jnp.concatenate([out[8 * b + i] for i in range(8)], axis=0) for b in range(4)]
    second = [found.astype(F32) for found in compress([gram[0], gram[3]])]
    for p in range(2):
        above[pl.ds(p * RANK, RANK), pl.ds(p * ROWS, ROWS)] = second[p]
    mixed = [
        jnp.concatenate([dot_nn(second[p], gram[2 * p + q]) for q in range(2)], axis=1)
        for p in range(2)
    ]
    last = compress([dot_nt(jnp.concatenate(mixed, axis=0), above[...])])[0]
    mix = dot_nn(last.astype(F32), above[...]).astype(BF16)
    for one in fetched:
        one.wait()
    weighted_out[...] = jnp.dot(mix, weighted_in[...], preferred_element_type=F32).astype(BF16)
    for one in moved:
        one.wait()
    rows_out[...] = jnp.dot(mix, rows_in[...], preferred_element_type=F32).astype(BF16)


def merge(gram, rows, weighted):
    shape = (32, PIECE, 128)
    vmem = pl.BlockSpec(memory_space=pltpu.VMEM)
    anywhere = pl.BlockSpec(memory_space=pl.ANY)
    return pl.pallas_call(
        merge_kernel,
        out_shape=(jax.ShapeDtypeStruct((RANK, SHARE), BF16),) * 2,
        in_specs=[vmem, anywhere, anywhere],
        out_specs=(vmem, vmem),
        scratch_shapes=[
            pltpu.VMEM(shape, F32),
            pltpu.VMEM((N_TM * RANK, SHARE), BF16),
            pltpu.VMEM((N_TM * RANK, SHARE), BF16),
            pltpu.VMEM((2 * RANK, 2 * ROWS), F32),
            pltpu.VMEM((31, PIECE, 128), F32),
            pltpu.VMEM((8, PIECE, 128), F32),
            pltpu.SemaphoreType.DMA((62,)),
            pltpu.SemaphoreType.DMA((62,)),
            pltpu.SemaphoreType.DMA((7,)),
            pltpu.SemaphoreType.DMA((7,)),
            pltpu.SemaphoreType.DMA((3,)),
            pltpu.SemaphoreType.DMA((3,)),
            pltpu.SemaphoreType.DMA((2,)),
        ],
        compiler_params=pltpu.CompilerParams(collective_id=1, has_side_effects=True),
        name="merge",
    )(gram.reshape(shape), rows, weighted)


def shards(snapshots, prior_basis, mass_factor, neighbours):
    tile = tiles_of(neighbours, lax.axis_index("space"))
    rows, weighted, gram = lowest(tile, prior_basis, snapshots, mass_factor)
    return merge(gram, rows, weighted)


def solution(mesh):
    return jax.shard_map(
        shards,
        mesh=mesh,
        in_specs=(P("tm", "space"), P("tm", "space"), P(None, None, "space"), P("space", None)),
        out_specs=(P(None, ("space", "tm")), P(None, ("space", "tm"))),
        check_vma=False,
    )
```

```python
import functools

import jax
import jax.numpy as jnp
from jax import lax
from jax.experimental import pallas as pl
from jax.experimental.pallas import tpu as pltpu
from jax.sharding import PartitionSpec as P

BLOCK = 64
RANK = 64
NEIGHBOURS = 7
REACH = 8
STEPS = 3
LOCAL_BLOCKS = 128
N_SPACE = 64
N_TM = 4
ROWS = 128
SLAB = LOCAL_BLOCKS * BLOCK
SHARE = SLAB // N_TM
HALO = REACH * BLOCK
WINDOW = SHARE + 2 * HALO
SHARE_BLOCKS = SHARE // BLOCK
TILES = WINDOW // 128
WIDE = SLAB + 2 * HALO
WIDE_TILES = WIDE // 128
HALO_TILES = HALO // 128
MESH = pl.DeviceIdType.MESH
HIGHEST = lax.Precision.HIGHEST
F32 = jnp.float32
BF16 = jnp.bfloat16


def dot_nn(a, b):
    return lax.dot_general(
        a, b, (((1,), (0,)), ((), ())), precision=HIGHEST, preferred_element_type=F32
    )


def dot_nt(a, b):
    return lax.dot_general(
        a, b, (((1,), (1,)), ((), ())), precision=HIGHEST, preferred_element_type=F32
    )


def eliminate(inners):
    sub = lax.broadcasted_iota(jnp.int32, (8, 128), 0)
    lane = lax.broadcasted_iota(jnp.int32, (8, 128), 1)
    grids = []
    for inner in inners:
        tiles = []
        for i in range(8):
            unit = jnp.where(lane == 8 * i + sub + BLOCK, 1.0, 0.0).astype(F32)
            left = jnp.concatenate([inner[8 * i : 8 * i + 8, :], jnp.zeros((8, BLOCK), F32)], axis=1)
            tiles.append(left + unit)
        grids.append(tiles)
    outs = [[] for _ in inners]
    for p in range(8):
        panels = [
            [[jnp.broadcast_to(tiles[i][:, 8 * p + q : 8 * p + q + 1], (8, 128)) for q in range(8)] for i in range(p, 8)]
            for tiles in grids
        ]
        roots = [jnp.ones((8, 128), F32) for _ in grids]
        for q in range(8):
            for m, (tiles, cols) in enumerate(zip(grids, panels)):
                pivot = jnp.broadcast_to(cols[0][q][q : q + 1, :], (8, 128))
                inv = 1.0 / pivot
                roots[m] = jnp.where(sub == q, pivot, roots[m])
                for r in range(q + 1, 8):
                    factor = jnp.broadcast_to(cols[0][r][q : q + 1, :], (8, 128)) * inv
                    for i in range(8 - p):
                        cols[i][r] = cols[i][r] - cols[i][q] * factor
                row = jnp.broadcast_to(tiles[p][q : q + 1, :], (8, 128)) * inv
                for i in range(p, 8):
                    change = cols[i - p][q] * row
                    if i == p:
                        change = jnp.where(sub > q, change, 0.0)
                    tiles[i] = tiles[i] - change
        for out, tiles, root in zip(outs, grids, roots):
            out.append(tiles[p] * lax.rsqrt(root))
    return [jnp.concatenate(out, axis=0) for out in outs]


def compress(grams):
    zeros = jnp.zeros((BLOCK, ROWS), F32)

    def apply(inverse, rows):
        return dot_nn(inverse, jnp.concatenate([zeros, rows], axis=0))

    def step(_, state):
        _, _, products = state
        seconds = [dot_nn(p, g) for p, g in zip(products, grams)]
        inverses = eliminate([dot_nt(p, q) for p, q in zip(products, seconds)])
        return inverses, products, [apply(inv, q) for inv, q in zip(inverses, seconds)]

    first = [gram[:RANK, :] for gram in grams]
    state = (first, first, first)
    for i in range(STEPS):
        state = step(i, state)
    inverses, products, nexts = state
    result = []
    for inv, p, q in zip(inverses, products, nexts):
        lengths = jnp.sqrt(jnp.sum(q * q, axis=1, keepdims=True) + 1e-06)
        result.append((apply(inv, p) * lengths).astype(BF16))
    return result


def tiles_of(neighbours, s):
    at = neighbours - (s * LOCAL_BLOCKS - REACH)
    second = lax.broadcasted_iota(jnp.int32, at.shape, 0) & 1
    moved = (at & 1) ^ second
    return ((at + 1 - second) >> 1) + moved * WIDE_TILES


def pick_modes(tile, j, tiles, in_low):
    picks = []
    for k in range(NEIGHBOURS):
        low = tiles[tile[2 * j, k]]
        high = tiles[tile[2 * j + 1, k]]
        picks.append(jnp.where(in_low, low, high))
    return jnp.concatenate(picks, axis=1)


def pick_factor(j, factor, in_low):
    zero = jnp.zeros((BLOCK, 128), BF16)
    pieces = []
    for k in range(NEIGHBOURS):
        block = factor[k, :, pl.ds(pl.multiple_of(j * 128, 128), 128)]
        pieces += [jnp.where(in_low, block, zero), jnp.where(in_low, zero, block)]
    return jnp.concatenate(pieces, axis=0)


def halves(before, after):
    return jnp.concatenate([before[:, BLOCK:], after[:, :BLOCK]], axis=1)


def widen(wide, tiles, low, high, unroll):
    def one_tile(m, carry):
        before = wide[:, pl.ds(pl.multiple_of(128 * (m - 1), 128), 128)]
        after = wide[:, pl.ds(pl.multiple_of(128 * m, 128), 128)]
        tiles[m] = after
        tiles[WIDE_TILES + m] = halves(before, after)
        return carry

    lax.fori_loop(low, high, one_tile, 0, unroll=unroll)


def widen_ends(wide, tiles):
    last = wide.shape[1] // 128 - 1
    first = wide[:, pl.ds(0, 128)]
    tiles[0] = first
    tiles[WIDE_TILES] = halves(first, first)
    end = wide[:, pl.ds(128 * last, 128)]
    tiles[WIDE_TILES + last + 1] = halves(end, end)


def whole_kernel(
    tile,
    prior,
    snaps,
    mass,
    rows_out,
    weighted_out,
    own,
    own_tiles,
    weights_own,
    weights_in,
    factor,
    gram,
    r_plane,
    r_z,
    total,
    coefs,
    basis_rows,
    rows_in,
    weighted,
    gram_all,
    r_wide,
    r_z_all,
    total_all,
    above,
    send_sem,
    recv_sem,
    local_sem,
    sum_send,
    sum_recv,
    wide_send,
    wide_recv,
    all_z_send,
    all_z_recv,
    rows_send,
    rows_recv,
):
    s = lax.axis_index("space")
    t = lax.axis_index("tm")
    c = lax.rem(s, 2)
    y = lax.rem(s // 2, 4)
    z = s // 8
    up = lax.rem(s + 1, N_SPACE)
    down = lax.rem(s + N_SPACE - 1, N_SPACE)
    sources = (prior, snaps)
    chunk = SLAB // 4

    def half(part):
        return pl.ds(part * 64, 64)

    loads = [
        pltpu.make_async_copy(
            sources[part], own.at[half(part), pl.ds(HALO, SLAB)], local_sem.at[part]
        )
        for part in range(2)
    ]
    fetches = [
        pltpu.make_async_copy(
            mass.at[:, :, pl.ds(chunk * i, chunk)],
            factor.at[:, :, pl.ds(chunk * i, chunk)],
            local_sem.at[2 + i],
        )
        for i in range(4)
    ]
    for one in loads + fetches:
        one.start()

    def space_of(zz, yy, cc):
        return zz * 8 + yy * 2 + cc

    x_peers = [(s, lax.rem(t + h, 4)) for h in (1, 2, 3)]
    me = c * 4 + y
    plane = []
    for dc, dy in ((1, 2), (0, 2), (1, 1), (1, 3), (0, 1), (0, 3), (1, 0)):
        pc, py = lax.rem(c + dc, 2), lax.rem(y + dy, 4)
        plane.append((pc * 4 + py, (space_of(z, py, pc), t)))
    z_peers = [(space_of(lax.rem(z + d, 8), y, c), t) for d in range(1, 8)]

    place = c * 16 + t * 4 + y
    hops = [(dc, dx, dy) for dx in (2, 1, 3, 0) for dy in (2, 1, 3, 0) for dc in (1, 0)]
    wide = []
    for dc, dx, dy in hops[:-1]:
        pc, px, py = lax.rem(c + dc, 2), lax.rem(t + dx, 4), lax.rem(y + dy, 4)
        wide.append((pc * 16 + px * 4 + py, (z * 8 + py * 2 + pc, px)))
    barrier = pltpu.get_barrier_semaphore()
    planes = [where for _, where in plane + wide]
    for peer in x_peers + planes + z_peers + [(up, t), (down, t)]:
        pl.semaphore_signal(barrier, inc=1, device_id=peer, device_id_type=MESH)

    pl.semaphore_wait(barrier, 50)

    def remote(src, dst, slot, peer, part):
        return pltpu.make_async_remote_copy(
            src_ref=src,
            dst_ref=dst,
            send_sem=send_sem.at[slot, part],
            recv_sem=recv_sem.at[slot, part],
            device_id=peer,
            device_id_type=MESH,
        )

    def share(hop):
        return remote(
            weights_own.at[:, pl.ds(pl.multiple_of(lax.rem(t + hop, 4) * SHARE, 128), SHARE)],
            weights_in.at[hop - 1],
            hop - 1,
            x_peers[hop - 1],
            0,
        )

    def own_edge(part, side):
        low, at = (SLAB - HALO, 0) if side == 0 else (0, WIDE - HALO)
        return remote(
            sources[part].at[:, pl.ds(low, HALO)],
            own.at[half(part), pl.ds(at, HALO)],
            3 + side,
            (up, t) if side == 0 else (down, t),
            part,
        )

    for part in range(2):
        for side in range(2):
            own_edge(part, side).start()

    in_low = lax.broadcasted_iota(jnp.int32, (1, 128), 1) < BLOCK
    for one in loads:
        one.wait()
    widen(own, own_tiles, HALO_TILES + 1, WIDE_TILES - HALO_TILES, 9)
    for part in range(2):
        for side in range(2):
            own_edge(part, side).wait()
    widen(own, own_tiles, 1, HALO_TILES + 1, HALO_TILES)
    widen(own, own_tiles, WIDE_TILES - HALO_TILES, WIDE_TILES, HALO_TILES)
    widen_ends(own, own_tiles)
    for one in fetches:
        one.wait()

    def own_quarter(quarter):
        def own_tile(i, carry):
            j = quarter * (SHARE_BLOCKS // 2) + i
            modes = pick_modes(tile, j, own_tiles, in_low)
            result = jnp.dot(modes, pick_factor(j, factor, in_low), preferred_element_type=F32)
            weights_own[:, pl.ds(pl.multiple_of(j * 128, 128), 128)] = result.astype(BF16)
            return carry

        lax.fori_loop(0, SHARE_BLOCKS // 2, own_tile, 0, unroll=4)

    for hop in (2, 1, 3):
        own_quarter(lax.rem(t + hop, 4))
        share(hop).start()
    own_quarter(t)
    local = lax.dot_general(
        weights_own[...], weights_own[...], (((1,), (1,)), ((), ())), preferred_element_type=F32
    )
    for i in range(8):
        gram[i] = local[16 * i : 16 * i + 16, :]

    def over(src, dst, slot, peer):
        return pltpu.make_async_remote_copy(
            src_ref=src,
            dst_ref=dst,
            send_sem=sum_send.at[slot],
            recv_sem=sum_recv.at[slot],
            device_id=peer,
            device_id_type=MESH,
        )

    def run(copies):
        for one in copies:
            one.start()
        for one in copies:
            one.wait()

    run([over(gram.at[owner], r_plane.at[i], i, where) for i, (owner, where) in enumerate(plane)])
    piece = gram[me]
    for i in range(7):
        piece = piece + r_plane[i]
    r_z[z] = piece
    run([over(r_z.at[z], r_z.at[z], 6 + d, z_peers[d - 1]) for d in (4, 3, 5, 2, 6, 1, 7)])
    piece = r_z[0]
    for i in range(1, 8):
        piece = piece + r_z[i]
    total[me] = piece
    run([over(total.at[me], total.at[me], 14 + i, where) for i, (_, where) in enumerate(plane)])

    summed = jnp.concatenate([total[i] for i in range(8)], axis=0)
    coefs[t] = compress([summed])[0]
    passed = [remote(coefs.at[t], coefs.at[t], 4 + h, x_peers[h - 1], 0) for h in (2, 1, 3)]
    for one in passed:
        one.start()

    basis_rows[...] = jnp.dot(
        coefs[t], own[:, pl.ds(HALO, SLAB)], preferred_element_type=F32
    ).astype(BF16)
    for hop in (1, 3, 2):
        share(hop).wait()

    def put(group, block):
        weighted[pl.ds(pl.multiple_of(group * RANK, RANK), RANK), :] = jnp.dot(
            coefs[group], block, preferred_element_type=F32
        ).astype(BF16)

    put(t, weights_own[:, pl.ds(pl.multiple_of(t * SHARE, 128), SHARE)])
    for one in passed:
        one.wait()
    for hop in (1, 2, 3):
        put(lax.rem(t + N_TM - hop, N_TM), weights_in[hop - 1])
    for a in range(2):
        for b in range(2):
            local = lax.dot_general(
                weighted[pl.ds(a * ROWS, ROWS), :],
                weighted[pl.ds(b * ROWS, ROWS), :],
                (((1,), (1,)), ((), ())),
                preferred_element_type=F32,
            )
            for i in range(8):
                gram_all[8 * (2 * a + b) + i] = local[16 * i : 16 * i + 16, :]

    def copy(src, dst, send, recv, slot, peer):
        return pltpu.make_async_remote_copy(
            src_ref=src,
            dst_ref=dst,
            send_sem=send.at[slot],
            recv_sem=recv.at[slot],
            device_id=peer,
            device_id_type=MESH,
        )

    run(
        [
            copy(gram_all.at[owner], r_wide.at[i], wide_send, wide_recv, i, where)
            for i, (owner, where) in enumerate(wide)
        ]
    )
    piece = gram_all[place]
    for i in range(31):
        piece = piece + r_wide[i]
    r_z_all[z] = piece
    run(
        [
            copy(r_z_all.at[z], r_z_all.at[z], all_z_send, all_z_recv, d - 1, z_peers[d - 1])
            for d in (4, 3, 5, 2, 6, 1, 7)
        ]
    )
    piece = r_z_all[0]
    for i in range(1, 8):
        piece = piece + r_z_all[i]
    total_all[place] = piece
    run(
        [
            copy(total_all.at[place], total_all.at[place], wide_send, wide_recv, 31 + i, where)
            for i, (_, where) in enumerate(wide)
        ]
    )

    own_rows = pl.ds(pl.multiple_of(t * RANK, RANK), RANK)

    def columns(member):
        return pl.ds(pl.multiple_of(member * SHARE, 128), SHARE)

    moved = [
        copy(
            basis_rows.at[:, columns(lax.rem(t + hop, 4))],
            rows_in.at[own_rows, :],
            rows_send,
            rows_recv,
            hop - 1,
            (s, lax.rem(t + hop, 4)),
        )
        for hop in (2, 1, 3)
    ]
    for one in moved:
        one.start()

    rows_in[own_rows, :] = basis_rows[:, columns(t)]
    above[...] = jnp.zeros_like(above)
    grams = [jnp.concatenate([total_all[8 * b + i] for i in range(8)], axis=0) for b in range(4)]
    second = [found.astype(F32) for found in compress([grams[0], grams[3]])]
    for p in range(2):
        above[pl.ds(p * RANK, RANK), pl.ds(p * ROWS, ROWS)] = second[p]
    mixed = [
        jnp.concatenate([dot_nn(second[p], grams[2 * p + q]) for q in range(2)], axis=1)
        for p in range(2)
    ]
    last = compress([dot_nt(jnp.concatenate(mixed, axis=0), above[...])])[0]
    mix = dot_nn(last.astype(F32), above[...]).astype(BF16)
    weighted_out[...] = jnp.dot(mix, weighted[...], preferred_element_type=F32).astype(BF16)
    for one in moved:
        one.wait()
    rows_out[...] = jnp.dot(mix, rows_in[...], preferred_element_type=F32).astype(BF16)


def merged(tile, prior, snaps, mass):
    piece = (16, 128)
    vmem = pl.BlockSpec(memory_space=pltpu.VMEM)
    anywhere = pl.BlockSpec(memory_space=pl.ANY)
    semaphores = [(8, 2), (8, 2), (6,), (21,), (21,), (62,), (62,), (7,), (7,), (3,), (3,)]
    return pl.pallas_call(
        whole_kernel,
        out_shape=(jax.ShapeDtypeStruct((RANK, SHARE), BF16),) * 2,
        in_specs=[pl.BlockSpec(memory_space=pltpu.SMEM), anywhere, anywhere, anywhere],
        out_specs=(vmem, vmem),
        scratch_shapes=[
            pltpu.VMEM((ROWS, WIDE), BF16),
            pltpu.VMEM((2 * WIDE_TILES + 1, ROWS, 128), BF16),
            pltpu.VMEM((ROWS, SLAB), BF16),
            pltpu.VMEM((3, ROWS, SHARE), BF16),
            pltpu.VMEM((NEIGHBOURS, BLOCK, SLAB), BF16),
            pltpu.VMEM((8,) + piece, F32),
            pltpu.VMEM((7,) + piece, F32),
            pltpu.VMEM((8,) + piece, F32),
            pltpu.VMEM((8,) + piece, F32),
            pltpu.VMEM((N_TM, RANK, ROWS), BF16),
            pltpu.VMEM((RANK, SLAB), BF16),
            pltpu.VMEM((N_TM * RANK, SHARE), BF16),
            pltpu.VMEM((N_TM * RANK, SHARE), BF16),
            pltpu.VMEM((32,) + piece, F32),
            pltpu.VMEM((31,) + piece, F32),
            pltpu.VMEM((8,) + piece, F32),
            pltpu.VMEM((32,) + piece, F32),
            pltpu.VMEM((2 * RANK, 2 * ROWS), F32),
        ]
        + [pltpu.SemaphoreType.DMA(shape) for shape in semaphores],
        compiler_params=pltpu.CompilerParams(collective_id=0, has_side_effects=True),
        name="merged",
    )(tile, prior, snaps, mass)


def pass_kernel(rows, weighted, rows_out, weighted_out):
    rows_out[...] = rows[...]
    weighted_out[...] = weighted[...]


def handed(rows, weighted):
    vmem = pl.BlockSpec(memory_space=pltpu.VMEM)
    return pl.pallas_call(
        pass_kernel,
        out_shape=(jax.ShapeDtypeStruct((RANK, SHARE), BF16),) * 2,
        in_specs=[vmem, vmem],
        out_specs=(vmem, vmem),
        name="handed",
    )(rows, weighted)


def shards(snapshots, prior_basis, mass_factor, neighbours):
    tile = tiles_of(neighbours, lax.axis_index("space"))
    return handed(*merged(tile, prior_basis, snapshots, mass_factor))


def solution(mesh):
    return jax.shard_map(
        shards,
        mesh=mesh,
        in_specs=(P("tm", "space"), P("tm", "space"), P(None, None, "space"), P("space", None)),
        out_specs=(P(None, ("space", "tm")), P(None, ("space", "tm"))),
        check_vma=False,
    )
```

```python
import functools

import jax
import jax.numpy as jnp
from jax import lax
from jax.experimental import pallas as pl
from jax.experimental.pallas import tpu as pltpu
from jax.sharding import PartitionSpec as P

BLOCK = 64
RANK = 64
NEIGHBOURS = 7
REACH = 8
STEPS = 3
LOCAL_BLOCKS = 128
N_SPACE = 64
N_TM = 4
ROWS = 128
SLAB = LOCAL_BLOCKS * BLOCK
SHARE = SLAB // N_TM
HALO = REACH * BLOCK
WINDOW = SHARE + 2 * HALO
SHARE_BLOCKS = SHARE // BLOCK
TILES = WINDOW // 128
WIDE = SLAB + 2 * HALO
WIDE_TILES = WIDE // 128
HALO_TILES = HALO // 128
MESH = pl.DeviceIdType.MESH
HIGHEST = lax.Precision.HIGHEST
F32 = jnp.float32
BF16 = jnp.bfloat16


def dot_nn(a, b):
    return lax.dot_general(
        a, b, (((1,), (0,)), ((), ())), precision=HIGHEST, preferred_element_type=F32
    )


def dot_nt(a, b):
    return lax.dot_general(
        a, b, (((1,), (1,)), ((), ())), precision=HIGHEST, preferred_element_type=F32
    )


def eliminate(inners):
    sub = lax.broadcasted_iota(jnp.int32, (8, 128), 0)
    lane = lax.broadcasted_iota(jnp.int32, (8, 128), 1)
    grids = []
    for inner in inners:
        tiles = []
        for i in range(8):
            unit = jnp.where(lane == 8 * i + sub + BLOCK, 1.0, 0.0).astype(F32)
            left = jnp.concatenate([inner[8 * i : 8 * i + 8, :], jnp.zeros((8, BLOCK), F32)], axis=1)
            tiles.append(left + unit)
        grids.append(tiles)
    outs = [[] for _ in inners]
    for p in range(8):
        panels = [
            [[jnp.broadcast_to(tiles[i][:, 8 * p + q : 8 * p + q + 1], (8, 128)) for q in range(8)] for i in range(p, 8)]
            for tiles in grids
        ]
        roots = [jnp.ones((8, 128), F32) for _ in grids]
        for q in range(8):
            for m, (tiles, cols) in enumerate(zip(grids, panels)):
                pivot = jnp.broadcast_to(cols[0][q][q : q + 1, :], (8, 128))
                inv = 1.0 / pivot
                roots[m] = jnp.where(sub == q, pivot, roots[m])
                for r in range(q + 1, 8):
                    factor = jnp.broadcast_to(cols[0][r][q : q + 1, :], (8, 128)) * inv
                    for i in range(8 - p):
                        cols[i][r] = cols[i][r] - cols[i][q] * factor
                row = jnp.broadcast_to(tiles[p][q : q + 1, :], (8, 128)) * inv
                for i in range(p, 8):
                    change = cols[i - p][q] * row
                    if i == p:
                        change = jnp.where(sub > q, change, 0.0)
                    tiles[i] = tiles[i] - change
        for out, tiles, root in zip(outs, grids, roots):
            out.append(tiles[p] * lax.rsqrt(root))
    return [jnp.concatenate(out, axis=0) for out in outs]


def compress(grams):
    zeros = jnp.zeros((BLOCK, ROWS), F32)

    def apply(inverse, rows):
        return dot_nn(inverse, jnp.concatenate([zeros, rows], axis=0))

    def step(_, state):
        _, _, products = state
        seconds = [dot_nn(p, g) for p, g in zip(products, grams)]
        inverses = eliminate([dot_nt(p, q) for p, q in zip(products, seconds)])
        return inverses, products, [apply(inv, q) for inv, q in zip(inverses, seconds)]

    first = [gram[:RANK, :] for gram in grams]
    state = (first, first, first)
    for i in range(STEPS):
        state = step(i, state)
    inverses, products, nexts = state
    result = []
    for inv, p, q in zip(inverses, products, nexts):
        lengths = jnp.sqrt(jnp.sum(q * q, axis=1, keepdims=True) + 1e-06)
        result.append((apply(inv, p) * lengths).astype(BF16))
    return result


def tiles_of(neighbours, s):
    at = neighbours.T - (s * LOCAL_BLOCKS - REACH)
    second = lax.broadcasted_iota(jnp.int32, at.shape, 1) & 1
    moved = (at & 1) ^ second
    return ((at + 1 - second) >> 1) + moved * WIDE_TILES


def pick_modes(tile, j, tiles, in_low):
    picks = []
    for k in range(NEIGHBOURS):
        low = tiles[tile[k, 2 * j]]
        high = tiles[tile[k, 2 * j + 1]]
        picks.append(jnp.where(in_low, low, high))
    return jnp.concatenate(picks, axis=1)


def pick_factor(j, factor, in_low):
    zero = jnp.zeros((BLOCK, 128), BF16)
    pieces = []
    for k in range(NEIGHBOURS):
        block = factor[k, :, pl.ds(pl.multiple_of(j * 128, 128), 128)]
        pieces += [jnp.where(in_low, block, zero), jnp.where(in_low, zero, block)]
    return jnp.concatenate(pieces, axis=0)


def halves(before, after):
    return jnp.concatenate([before[:, BLOCK:], after[:, :BLOCK]], axis=1)


def widen(wide, tiles, low, high, unroll):
    def one_tile(m, carry):
        before = wide[:, pl.ds(pl.multiple_of(128 * (m - 1), 128), 128)]
        after = wide[:, pl.ds(pl.multiple_of(128 * m, 128), 128)]
        tiles[m] = after
        tiles[WIDE_TILES + m] = halves(before, after)
        return carry

    lax.fori_loop(low, high, one_tile, 0, unroll=unroll)


def widen_ends(wide, tiles):
    last = wide.shape[1] // 128 - 1
    first = wide[:, pl.ds(0, 128)]
    tiles[0] = first
    tiles[WIDE_TILES] = halves(first, first)
    end = wide[:, pl.ds(128 * last, 128)]
    tiles[WIDE_TILES + last + 1] = halves(end, end)


def whole_kernel(
    tile,
    prior,
    snaps,
    mass,
    rows_out,
    weighted_out,
    own,
    own_tiles,
    weights_own,
    weights_in,
    factor,
    gram,
    r_plane,
    r_z,
    total,
    coefs,
    basis_rows,
    rows_in,
    weighted,
    gram_all,
    r_wide,
    r_z_all,
    total_all,
    above,
    send_sem,
    recv_sem,
    local_sem,
    sum_send,
    sum_recv,
    wide_send,
    wide_recv,
    all_z_send,
    all_z_recv,
    rows_send,
    rows_recv,
):
    s = lax.axis_index("space")
    t = lax.axis_index("tm")
    c = lax.rem(s, 2)
    y = lax.rem(s // 2, 4)
    z = s // 8
    up = lax.rem(s + 1, N_SPACE)
    down = lax.rem(s + N_SPACE - 1, N_SPACE)
    sources = (prior, snaps)
    chunk = SLAB // 4

    def half(part):
        return pl.ds(part * 64, 64)

    loads = [
        pltpu.make_async_copy(
            sources[part], own.at[half(part), pl.ds(HALO, SLAB)], local_sem.at[part]
        )
        for part in range(2)
    ]
    fetches = [
        pltpu.make_async_copy(
            mass.at[:, :, pl.ds(chunk * i, chunk)],
            factor.at[:, :, pl.ds(chunk * i, chunk)],
            local_sem.at[2 + i],
        )
        for i in (1, 2, 0, 3)
    ]
    for one in loads + fetches:
        one.start()

    def space_of(zz, yy, cc):
        return zz * 8 + yy * 2 + cc

    x_peers = [(s, lax.rem(t + h, 4)) for h in (1, 2, 3)]
    me = c * 4 + y
    plane = []
    for dc, dy in ((1, 2), (0, 2), (1, 1), (1, 3), (0, 1), (0, 3), (1, 0)):
        pc, py = lax.rem(c + dc, 2), lax.rem(y + dy, 4)
        plane.append((pc * 4 + py, (space_of(z, py, pc), t)))
    z_peers = [(space_of(lax.rem(z + d, 8), y, c), t) for d in range(1, 8)]

    place = c * 16 + t * 4 + y
    hops = [(dc, dx, dy) for dx in (2, 1, 3, 0) for dy in (2, 1, 3, 0) for dc in (1, 0)]
    wide = []
    for dc, dx, dy in hops[:-1]:
        pc, px, py = lax.rem(c + dc, 2), lax.rem(t + dx, 4), lax.rem(y + dy, 4)
        wide.append((pc * 16 + px * 4 + py, (z * 8 + py * 2 + pc, px)))
    barrier = pltpu.get_barrier_semaphore()
    planes = [where for _, where in plane + wide]
    for peer in x_peers + planes + z_peers + [(up, t), (down, t)]:
        pl.semaphore_signal(barrier, inc=1, device_id=peer, device_id_type=MESH)

    pl.semaphore_wait(barrier, 50)

    def remote(src, dst, slot, peer, part):
        return pltpu.make_async_remote_copy(
            src_ref=src,
            dst_ref=dst,
            send_sem=send_sem.at[slot, part],
            recv_sem=recv_sem.at[slot, part],
            device_id=peer,
            device_id_type=MESH,
        )

    def share(hop):
        target = lax.rem(t + hop, 4)
        return remote(
            weights_own.at[:, pl.ds(pl.multiple_of(target * SHARE, 128), SHARE)],
            weights_in.at[hop - 1],
            hop - 1,
            (s, target),
            0,
        )

    def own_edge(part, side):
        low, at = (SLAB - HALO, 0) if side == 0 else (0, WIDE - HALO)
        return remote(
            sources[part].at[:, pl.ds(low, HALO)],
            own.at[half(part), pl.ds(at, HALO)],
            3 + side,
            (up, t) if side == 0 else (down, t),
            part,
        )

    for part in range(2):
        for side in range(2):
            own_edge(part, side).start()

    in_low = lax.broadcasted_iota(jnp.int32, (1, 128), 1) < BLOCK
    for one in loads:
        one.wait()
    widen(own, own_tiles, HALO_TILES + 1, WIDE_TILES - HALO_TILES, 9)
    def own_quarter(quarter):
        def own_tile(i, carry):
            j = quarter * (SHARE_BLOCKS // 2) + i
            modes = pick_modes(tile, j, own_tiles, in_low)
            result = jnp.dot(modes, pick_factor(j, factor, in_low), preferred_element_type=F32)
            weights_own[:, pl.ds(pl.multiple_of(j * 128, 128), 128)] = result.astype(BF16)
            return carry

        lax.fori_loop(0, SHARE_BLOCKS // 2, own_tile, 0, unroll=4)

    def send_quarter(quarter):
        for g in range(N_TM):
            if g != quarter:

                @pl.when(t == g)
                def _():
                    share((quarter - g) % N_TM).start()

    for at, quarter in enumerate((1, 2, 0, 3)):
        if at == 2:
            for part in range(2):
                for side in range(2):
                    own_edge(part, side).wait()
            widen(own, own_tiles, 1, HALO_TILES + 1, HALO_TILES)
            widen(own, own_tiles, WIDE_TILES - HALO_TILES, WIDE_TILES, HALO_TILES)
            widen_ends(own, own_tiles)
        fetches[at].wait()
        own_quarter(quarter)
        send_quarter(quarter)
    local = lax.dot_general(
        weights_own[...], weights_own[...], (((1,), (1,)), ((), ())), preferred_element_type=F32
    )
    for i in range(8):
        gram[i] = local[16 * i : 16 * i + 16, :]

    def over(src, dst, slot, peer):
        return pltpu.make_async_remote_copy(
            src_ref=src,
            dst_ref=dst,
            send_sem=sum_send.at[slot],
            recv_sem=sum_recv.at[slot],
            device_id=peer,
            device_id_type=MESH,
        )

    def run(copies):
        for one in copies:
            one.start()
        for one in copies:
            one.wait()

    run([over(gram.at[owner], r_plane.at[i], i, where) for i, (owner, where) in enumerate(plane)])
    piece = gram[me]
    for i in range(7):
        piece = piece + r_plane[i]
    r_z[z] = piece
    run([over(r_z.at[z], r_z.at[z], 6 + d, z_peers[d - 1]) for d in (4, 3, 5, 2, 6, 1, 7)])
    piece = r_z[0]
    for i in range(1, 8):
        piece = piece + r_z[i]
    total[me] = piece
    run([over(total.at[me], total.at[me], 14 + i, where) for i, (_, where) in enumerate(plane)])

    summed = jnp.concatenate([total[i] for i in range(8)], axis=0)
    coefs[t] = compress([summed])[0]
    passed = [remote(coefs.at[t], coefs.at[t], 4 + h, x_peers[h - 1], 0) for h in (2, 1, 3)]
    for one in passed:
        one.start()

    basis_rows[...] = jnp.dot(
        coefs[t], own[:, pl.ds(HALO, SLAB)], preferred_element_type=F32
    ).astype(BF16)
    for hop in (1, 3, 2):
        share(hop).wait()

    def put(group, block):
        weighted[pl.ds(pl.multiple_of(group * RANK, RANK), RANK), :] = jnp.dot(
            coefs[group], block, preferred_element_type=F32
        ).astype(BF16)

    put(t, weights_own[:, pl.ds(pl.multiple_of(t * SHARE, 128), SHARE)])
    for one in passed:
        one.wait()
    for hop in (1, 2, 3):
        put(lax.rem(t + N_TM - hop, N_TM), weights_in[hop - 1])
    for a in range(2):
        for b in range(2):
            local = lax.dot_general(
                weighted[pl.ds(a * ROWS, ROWS), :],
                weighted[pl.ds(b * ROWS, ROWS), :],
                (((1,), (1,)), ((), ())),
                preferred_element_type=F32,
            )
            for i in range(8):
                gram_all[8 * (2 * a + b) + i] = local[16 * i : 16 * i + 16, :]

    def copy(src, dst, send, recv, slot, peer):
        return pltpu.make_async_remote_copy(
            src_ref=src,
            dst_ref=dst,
            send_sem=send.at[slot],
            recv_sem=recv.at[slot],
            device_id=peer,
            device_id_type=MESH,
        )

    run(
        [
            copy(gram_all.at[owner], r_wide.at[i], wide_send, wide_recv, i, where)
            for i, (owner, where) in enumerate(wide)
        ]
    )
    piece = gram_all[place]
    for i in range(31):
        piece = piece + r_wide[i]
    r_z_all[z] = piece
    run(
        [
            copy(r_z_all.at[z], r_z_all.at[z], all_z_send, all_z_recv, d - 1, z_peers[d - 1])
            for d in (4, 3, 5, 2, 6, 1, 7)
        ]
    )
    piece = r_z_all[0]
    for i in range(1, 8):
        piece = piece + r_z_all[i]
    total_all[place] = piece
    run(
        [
            copy(total_all.at[place], total_all.at[place], wide_send, wide_recv, 31 + i, where)
            for i, (_, where) in enumerate(wide)
        ]
    )

    own_rows = pl.ds(pl.multiple_of(t * RANK, RANK), RANK)

    def columns(member):
        return pl.ds(pl.multiple_of(member * SHARE, 128), SHARE)

    moved = [
        copy(
            basis_rows.at[:, columns(lax.rem(t + hop, 4))],
            rows_in.at[own_rows, :],
            rows_send,
            rows_recv,
            hop - 1,
            (s, lax.rem(t + hop, 4)),
        )
        for hop in (2, 1, 3)
    ]
    for one in moved:
        one.start()

    rows_in[own_rows, :] = basis_rows[:, columns(t)]
    above[...] = jnp.zeros_like(above)
    grams = [jnp.concatenate([total_all[8 * b + i] for i in range(8)], axis=0) for b in range(4)]
    second = [found.astype(F32) for found in compress([grams[0], grams[3]])]
    for p in range(2):
        above[pl.ds(p * RANK, RANK), pl.ds(p * ROWS, ROWS)] = second[p]
    mixed = [
        jnp.concatenate([dot_nn(second[p], grams[2 * p + q]) for q in range(2)], axis=1)
        for p in range(2)
    ]
    last = compress([dot_nt(jnp.concatenate(mixed, axis=0), above[...])])[0]
    mix = dot_nn(last.astype(F32), above[...]).astype(BF16)
    weighted_out[...] = jnp.dot(mix, weighted[...], preferred_element_type=F32).astype(BF16)
    for one in moved:
        one.wait()
    rows_out[...] = jnp.dot(mix, rows_in[...], preferred_element_type=F32).astype(BF16)


def merged(tile, prior, snaps, mass):
    piece = (16, 128)
    vmem = pl.BlockSpec(memory_space=pltpu.VMEM)
    anywhere = pl.BlockSpec(memory_space=pl.ANY)
    semaphores = [(8, 2), (8, 2), (6,), (21,), (21,), (62,), (62,), (7,), (7,), (3,), (3,)]
    return pl.pallas_call(
        whole_kernel,
        out_shape=(jax.ShapeDtypeStruct((RANK, SHARE), BF16),) * 2,
        in_specs=[pl.BlockSpec(memory_space=pltpu.SMEM), anywhere, anywhere, anywhere],
        out_specs=(vmem, vmem),
        scratch_shapes=[
            pltpu.VMEM((ROWS, WIDE), BF16),
            pltpu.VMEM((2 * WIDE_TILES + 1, ROWS, 128), BF16),
            pltpu.VMEM((ROWS, SLAB), BF16),
            pltpu.VMEM((3, ROWS, SHARE), BF16),
            pltpu.VMEM((NEIGHBOURS, BLOCK, SLAB), BF16),
            pltpu.VMEM((8,) + piece, F32),
            pltpu.VMEM((7,) + piece, F32),
            pltpu.VMEM((8,) + piece, F32),
            pltpu.VMEM((8,) + piece, F32),
            pltpu.VMEM((N_TM, RANK, ROWS), BF16),
            pltpu.VMEM((RANK, SLAB), BF16),
            pltpu.VMEM((N_TM * RANK, SHARE), BF16),
            pltpu.VMEM((N_TM * RANK, SHARE), BF16),
            pltpu.VMEM((32,) + piece, F32),
            pltpu.VMEM((31,) + piece, F32),
            pltpu.VMEM((8,) + piece, F32),
            pltpu.VMEM((32,) + piece, F32),
            pltpu.VMEM((2 * RANK, 2 * ROWS), F32),
        ]
        + [pltpu.SemaphoreType.DMA(shape) for shape in semaphores],
        compiler_params=pltpu.CompilerParams(collective_id=0, has_side_effects=True),
        name="merged",
    )(tile, prior, snaps, mass)


def pass_kernel(rows, weighted, rows_out, weighted_out):
    rows_out[...] = rows[...]
    weighted_out[...] = weighted[...]


def handed(rows, weighted):
    vmem = pl.BlockSpec(memory_space=pltpu.VMEM)
    return pl.pallas_call(
        pass_kernel,
        out_shape=(jax.ShapeDtypeStruct((RANK, SHARE), BF16),) * 2,
        in_specs=[vmem, vmem],
        out_specs=(vmem, vmem),
        name="handed",
    )(rows, weighted)


def shards(snapshots, prior_basis, mass_factor, neighbours):
    tile = tiles_of(neighbours, lax.axis_index("space"))
    return handed(*merged(tile, prior_basis, snapshots, mass_factor))


def solution(mesh):
    return jax.shard_map(
        shards,
        mesh=mesh,
        in_specs=(P("tm", "space"), P("tm", "space"), P(None, None, "space"), P("space", None)),
        out_specs=(P(None, ("space", "tm")), P(None, ("space", "tm"))),
        check_vma=False,
    )
```
